32 devices in a mesh: chan: 8 (over z, y), tm: 4 (over x, core).
Axes of the slice: x: 2, y: 2, z: 4, core: 2. Of those that a mesh axis runs over, the one named last changes fastest.
Arguments:
- filterbank: bfloat16 [4096, 32768], P('chan', 'tm'), may hold values from -6 to 6
- chan_delay: int32 [4096], P('chan'), may hold values from 0 to 128, as said below
- sub_delay: int32 [64, 64], replicated, may hold values from 0 to 896, as said below
- box_width: int32 [4], replicated, may hold values from 1 to 32, as said below
Outputs:
- ffa_out: float32 [64, 16, 2048], P('chan', None, 'tm')
- box_out: float32 [64, 16, 4, 2048], P('chan', None, None, 'tm')
The draws below stay inside these ranges and needn't reach their ends.
Inputs may be any that keep to these rules, and one draw needn't show every extreme that they name: `chan_delay`: the value 128 occurs in every draw. `sub_delay`: the value 896 occurs in every draw. `box_width`: the value 32 occurs in every draw.
All inputs are finite; a program needn't handle non-finite values.
Results may differ from the reference program's by a relative error of at most 0.0003.
Values may be sent and summed in bfloat16 or wider, within the bound.
No kernel may reach another device: no remote copies, remote signals or barrier semaphores. Data moves between devices by JAX's collectives and lax.ppermute only.
A program may use at most 128 MiB of HBM per device.

```python
import math
import jax
import jax.numpy as jnp
from jax import lax

NCHAN = 4096
NSUB = 64
NDM = 64
NBIN = 2048
LEVELS = 4
MAXW = 32
NWID = 4
D1MAX = 128
D2MAX = 896
TOTAL = 32768


def draw_chan_delay(key, part):
    first, second = jax.random.split(jax.random.fold_in(key, 11))
    values = jax.random.randint(first, (NCHAN,), 0, D1MAX + 1)
    where_top = jax.random.randint(second, (), 0, NCHAN)
    return jnp.where(jnp.arange(NCHAN) == where_top, D1MAX, values).astype(jnp.int32)


def draw_sub_delay(key, part):
    first, second = jax.random.split(jax.random.fold_in(key, 23))
    values = jax.random.randint(first, (NDM * NSUB,), 0, D2MAX + 1)
    where_top = jax.random.randint(second, (), 0, NDM * NSUB)
    values = jnp.where(jnp.arange(NDM * NSUB) == where_top, D2MAX, values)
    return values.reshape(NDM, NSUB).astype(jnp.int32)


def draw_box_width(key, part):
    first, second = jax.random.split(jax.random.fold_in(key, 37))
    values = jax.random.randint(first, (NWID,), 1, MAXW + 1)
    where_top = jax.random.randint(second, (), 0, NWID)
    return jnp.where(jnp.arange(NWID) == where_top, MAXW, values).astype(jnp.int32)


def shard_levels(stream_key, extent, cuts, smallest, largest):
    loudness, own = 1.0, jax.random.fold_in(stream_key, 6)
    for axis_at, shards_of in cuts:
        steps = jnp.exp(jax.random.uniform(jax.random.fold_in(own, axis_at), (shards_of,), jnp.float32, smallest / len(cuts), largest / len(cuts)))
        loudness = loudness * jnp.repeat(steps, extent[axis_at] // shards_of).reshape([-1 if axis == axis_at else 1 for axis in range(len(extent))])
    return loudness


def gaussian(key, dims, spread, bound, cuts=(), held_as=jnp.bfloat16):
    drawn = spread * jax.random.normal(key, dims, jnp.float32)
    if cuts:
        drawn = drawn * shard_levels(key, dims, cuts, -0.22, 0.18)
    return jnp.clip(drawn, -bound, bound).astype(held_as)


def setup_inputs(seed: int = 0) -> dict:
    streams_of = jax.random.split(jax.random.key(seed), 5)
    filterbank = gaussian(streams_of[0], (NCHAN, TOTAL), 1.0, 6.0, ((0, 8), (1, 4)))
    chan_delay = draw_chan_delay(jax.random.fold_in(streams_of[4], 71), 0)
    sub_delay = draw_sub_delay(jax.random.fold_in(streams_of[4], 71), 0)
    box_width = draw_box_width(jax.random.fold_in(streams_of[4], 71), 0)
    return {"filterbank": filterbank, "chan_delay": chan_delay, "sub_delay": sub_delay, "box_width": box_width}


def reference(filterbank, chan_delay, sub_delay, box_width):
    sample_total = filterbank.shape[1]
    rim_cols = D1MAX + D2MAX
    padded = jnp.pad(filterbank, ((0, 0), (0, rim_cols)))
    sample_span = sample_total + D2MAX
    chan_per_sub = NCHAN // NSUB

    def sum_subband(inputs):
        chan_rows, chan_shift = inputs
        pieces = jax.vmap(lambda r, d: lax.dynamic_slice_in_dim(r, d, sample_span))(chan_rows, chan_shift)
        return lax.optimization_barrier(jnp.sum(pieces.astype(jnp.float32), axis=0))
    subbands = lax.map(sum_subband, (padded.reshape(NSUB, chan_per_sub, sample_total + rim_cols), chan_delay.reshape(NSUB, chan_per_sub)))

    def sum_trial(trial_shift):
        pieces = jax.vmap(lambda r, d: lax.dynamic_slice_in_dim(r, d, sample_total))(subbands, trial_shift)
        return lax.optimization_barrier(jnp.sum(pieces, axis=0)) / math.sqrt(NCHAN)
    series = lax.map(sum_trial, sub_delay)
    row_count = sample_total // NBIN
    profiles = series.reshape(NDM, row_count, NBIN)
    for level_idx in range(LEVELS):
        half_rows = 2 ** level_idx
        blocks = profiles.reshape(NDM, row_count // (2 * half_rows), 2, half_rows, NBIN)
        upper_half = blocks[:, :, 0]
        lower_half = blocks[:, :, 1]
        stacked_rows = []
        for j in range(2 * half_rows):
            stacked_rows.append(upper_half[:, :, j // 2] + jnp.roll(lower_half[:, :, j // 2], -((j + 1) // 2), axis=-1))
        profiles = jnp.stack(stacked_rows, axis=2).reshape(NDM, row_count, NBIN)
    ffa_out = profiles * 2.0 ** (-LEVELS / 2)
    boxcar_sum = jnp.zeros((NDM, row_count, NWID, NBIN), jnp.float32)
    for i in range(MAXW):
        active = (box_width > i).astype(jnp.float32)
        boxcar_sum = boxcar_sum + active[:, None] * jnp.roll(ffa_out, -i, axis=-1)[:, :, None, :]
    box_out = boxcar_sum / jnp.sqrt(box_width.astype(jnp.float32))[:, None]
    return (ffa_out, box_out)
```

```python
import functools
import math

import jax
import jax.numpy as jnp
from jax import lax
from jax.experimental import pallas as pl
from jax.experimental.pallas import tpu as pltpu
from jax.sharding import PartitionSpec as P

NCHAN = 4096
NSUB = 64
NDM = 64
NBIN = 2048
LEVELS = 4
MAXW = 32
D1MAX = 128
D2MAX = 896

LANES = 128
F32 = jnp.float32
GROUP = 2**LEVELS
ROW_BLOCKS = NBIN // LANES
LEAD = (D1MAX + D2MAX) // LANES
VMEM_LIMIT = 48 << 20
SCALE = 2.0 ** (-LEVELS / 2) / math.sqrt(NCHAN)


def lane_iota(rows):
    return lax.broadcasted_iota(jnp.int32, (rows, LANES), 1)


def column_exponent(peak):
    return jnp.floor(jnp.log2(jnp.maximum(peak, 2.0**-110))) - 14.0


def scaled(values, exponent):
    return jnp.clip(jnp.round(values * jnp.exp2(-exponent)), -32767.0, 32767.0)


def to_i16(values):
    return values.astype(jnp.int32).astype(jnp.int16)


def pairs(size, flip):
    return [(i, i ^ flip) for i in range(size)]


def subband_kernel(chans, blocks, subs, delay_ref, x_ref, out_ref, sums):
    sub = pl.program_id(0)
    lane = lane_iota(8)
    row = lax.broadcasted_iota(jnp.int32, (8, LANES), 0)
    tiles = chans // 8
    where_from, from_next = [], []
    for tile in range(tiles):
        delay = jnp.zeros((8, LANES), jnp.int32)
        for i in range(8):
            delay = jnp.where(row == i, delay_ref[sub * chans + tile * 8 + i], delay)
        where_from.append((lane + delay) & (LANES - 1))
        from_next.append(lane < delay)

    def load(block):
        loaded = []
        for pair in range(tiles // 2):
            both = x_ref[16 * pair : 16 * pair + 16, block * LANES : (block + 1) * LANES]
            both = both.astype(F32)
            loaded += [both[:8], both[8:]]
        return loaded

    def emit(block, here, after):
        terms = []
        for tile in range(tiles):
            mixed = jnp.where(from_next[tile], after[tile], here[tile])
            terms.append(
                jnp.take_along_axis(
                    mixed, where_from[tile], axis=1, mode="promise_in_bounds"
                )
            )
        while len(terms) > 1:
            terms = [a + b for a, b in zip(terms[::2], terms[1::2])]
        total = jnp.sum(terms[0], axis=0, keepdims=True)
        sums[pl.ds((block + 1) * subs + sub, 1), :] = total

    zero = [jnp.zeros((8, LANES), F32)] * tiles
    here = zero
    for block in range(-1, blocks):
        after = load(block + 1) if block + 1 < blocks else zero
        emit(block, here, after)
        here = after

    @pl.when(sub == subs - 1)
    def _():
        rows = (blocks + 1) * subs
        values = sums[...].reshape(blocks + 1, subs, LANES)
        exponent = column_exponent(jnp.max(jnp.abs(values), axis=0))
        out_ref[0:rows, :] = to_i16(scaled(values, exponent[None]).reshape(rows, LANES))
        out_ref[rows : rows + subs, :] = to_i16(exponent)


def subband_sums(filterbank, chan_delay, subs):
    chans_here, samples = filterbank.shape
    chans, blocks = chans_here // subs, samples // LANES
    rows = (blocks + 2) * subs
    return pl.pallas_call(
        functools.partial(subband_kernel, chans, blocks, subs),
        grid=(subs,),
        in_specs=[
            pl.BlockSpec(memory_space=pltpu.SMEM),
            pl.BlockSpec((chans, samples), lambda i: (i, 0)),
        ],
        out_specs=pl.BlockSpec((rows, LANES), lambda i: (0, 0)),
        out_shape=jax.ShapeDtypeStruct((rows, LANES), jnp.int16),
        scratch_shapes=[pltpu.VMEM(((blocks + 1) * subs, LANES), F32)],
        compiler_params=pltpu.CompilerParams(vmem_limit_bytes=VMEM_LIMIT),
        name="subbands",
    )(chan_delay, filterbank)


def trial_kernel(blocks, subs, trials, flips, coded, n_in, delay_ref, *refs):
    parts, outs = refs[:n_in], refs[n_in : n_in + len(flips)]
    spread, acc = refs[n_in + len(flips) :]
    chan = lax.axis_index("chan")
    out_blocks = LEAD + blocks
    depth = out_blocks + LEAD + 1
    for at, part in enumerate(parts):
        base = at * depth * subs
        rows = (blocks + 1) * subs
        scale = jnp.exp2(part[rows : rows + subs, :].astype(F32))
        lead = (LEAD - 1) * subs
        spread[base : base + lead, :] = jnp.zeros((lead, LANES), F32)
        tail = base + lead + rows
        spread[tail : base + depth * subs, :] = jnp.zeros(
            (depth * subs - lead - rows, LANES), F32
        )
        values = part[0:rows, :].astype(F32).reshape(blocks + 1, subs, LANES)
        spread[base + lead : tail, :] = (values * scale[None]).reshape(rows, LANES)

    lane = lane_iota(out_blocks)

    def one_trial(trial, owner, out):
        total = jnp.zeros((out_blocks, LANES), F32)
        for at in range(n_in):
            for sub in range(subs):
                delay = delay_ref[owner * trials + trial, (chan ^ at) * subs + sub]
                shift = delay & (LANES - 1)
                first = at * depth * subs + (delay >> 7) * subs + sub
                here = spread[pl.ds(first, out_blocks, stride=subs), :]
                after = spread[pl.ds(first + subs, out_blocks, stride=subs), :]
                mixed = jnp.where(lane < shift, after, here)
                total = total + pltpu.roll(mixed, (LANES - shift) & (LANES - 1), 1)
        out[pl.ds(trial, out_blocks, stride=trials), :] = total

    rows = out_blocks * trials
    for flip, out in zip(flips, outs):
        target = acc if coded else out

        @pl.loop(0, trials)
        def _(trial):
            one_trial(trial, chan ^ flip, target)

        if coded:
            values = acc[...].reshape(out_blocks, trials, LANES)
            exponent = column_exponent(jnp.max(jnp.abs(values), axis=0))
            out[0:rows, :] = to_i16(
                scaled(values, exponent[None]).reshape(rows, LANES)
            )
            out[rows : rows + trials, :] = to_i16(exponent)


def trial_sums(parts, sub_delay, blocks, subs, trials, flips, coded):
    out_blocks = LEAD + blocks
    depth = out_blocks + LEAD + 1
    rows = out_blocks * trials
    out = jax.ShapeDtypeStruct(
        (rows + trials if coded else rows, LANES), jnp.int16 if coded else F32
    )
    vmem = pl.BlockSpec(memory_space=pltpu.VMEM)
    return pl.pallas_call(
        functools.partial(
            trial_kernel, blocks, subs, trials, flips, coded, len(parts)
        ),
        in_specs=[pl.BlockSpec(memory_space=pltpu.SMEM)] + [vmem] * len(parts),
        out_specs=[vmem] * len(flips),
        out_shape=[out] * len(flips),
        scratch_shapes=[
            pltpu.VMEM((len(parts) * depth * subs, LANES), F32),
            pltpu.VMEM((rows, LANES), F32),
        ],
        compiler_params=pltpu.CompilerParams(vmem_limit_bytes=VMEM_LIMIT),
        name="trials_coded" if coded else "trials",
    )(sub_delay, *parts)


def cut_kernel(blocks, trials, owners, n_far, own_ref, *refs):
    far, mine, sends = refs[:n_far], refs[n_far], refs[n_far + 1 : n_far + owners]
    series, whole, piece = refs[n_far + owners :]
    here = lax.axis_index("tm")
    out_blocks = LEAD + blocks
    rows = out_blocks * trials
    total = own_ref[...].reshape(out_blocks, trials, LANES)
    for part in far:
        scale = jnp.exp2(part[rows : rows + trials, :].astype(F32))
        values = part[0:rows, :].astype(F32).reshape(out_blocks, trials, LANES)
        total = total + values * scale[None]
    total = total * SCALE
    ahead = (ROW_BLOCKS - LEAD) * trials
    exponent = column_exponent(jnp.max(jnp.abs(total), axis=0))
    for target, values in ((series, total), (whole, scaled(total, exponent[None]))):
        target[0:ahead, :] = jnp.zeros((ahead, LANES), F32)
        target[ahead : ahead + rows, :] = values.reshape(rows, LANES)
    periods = blocks // ROW_BLOCKS
    bin_blocks = ROW_BLOCKS // owners
    for flip in range(owners):
        source, target = (series, mine) if flip == 0 else (whole, piece)
        at = 0
        for period in range(periods + 1):
            for j in range(bin_blocks + 1):
                block = ((here ^ flip) * bin_blocks + j) & (ROW_BLOCKS - 1)
                first = (period * ROW_BLOCKS + block) * trials
                target[at : at + trials, :] = source[pl.ds(first, trials), :]
                at += trials
        if flip:
            sends[flip - 1][0:at, :] = to_i16(piece[...])
            sends[flip - 1][at : at + trials, :] = to_i16(exponent)


def cut_by_phase(own, far, blocks, trials, owners):
    out_blocks = LEAD + blocks
    periods = blocks // ROW_BLOCKS
    bin_blocks = ROW_BLOCKS // owners
    rows = (periods + 1) * (bin_blocks + 1) * trials
    vmem = pl.BlockSpec(memory_space=pltpu.VMEM)
    held = (out_blocks + ROW_BLOCKS - LEAD) * trials
    return pl.pallas_call(
        functools.partial(cut_kernel, blocks, trials, owners, len(far)),
        in_specs=[vmem] * (1 + len(far)),
        out_specs=[vmem] * owners,
        out_shape=[jax.ShapeDtypeStruct((rows, LANES), F32)]
        + [jax.ShapeDtypeStruct((rows + trials, LANES), jnp.int16)] * (owners - 1),
        scratch_shapes=[
            pltpu.VMEM((held, LANES), F32),
            pltpu.VMEM((held, LANES), F32),
            pltpu.VMEM((rows, LANES), F32),
        ],
        compiler_params=pltpu.CompilerParams(vmem_limit_bytes=VMEM_LIMIT),
        name="cut",
    )(own, *far)


def fold_kernel(periods, trials, owners, widths, width_ref, mine_ref, *refs):
    parts, (ffa_ref, box_ref) = refs[: owners - 1], refs[owners - 1 : owners + 1]
    rows_in, code, folded = refs[owners + 1 :]
    here = lax.axis_index("tm")
    bin_blocks = ROW_BLOCKS // owners
    row_len = (bin_blocks + 1) * trials
    held = periods * row_len
    rows_in[0:row_len, :] = jnp.zeros((row_len, LANES), F32)
    for flip in range(owners):
        if flip == 0:
            rest = mine_ref[row_len : row_len + held, :]
        else:
            part = parts[flip - 1]
            total = row_len + held
            scale = jnp.exp2(part[total : total + trials, :].astype(F32))
            values = part[0:total, :].astype(F32)
            values = values.reshape(total // trials, trials, LANES) * scale[None]
            code[flip - 1] = values.reshape(total, LANES)
            rest = code[flip - 1, row_len : row_len + held, :]
        first = (here ^ flip) * held + row_len
        rows_in[pl.ds(first, held), :] = rest
    for flip in range(owners):
        early = mine_ref[0:row_len, :] if flip == 0 else code[flip - 1, 0:row_len, :]
        first = (here ^ flip) * held
        rows_in[pl.ds(first, row_len), :] += early

    tap = lax.broadcasted_iota(jnp.int32, (2 * LANES, LANES), 0) - lax.broadcasted_iota(
        jnp.int32, (2 * LANES, LANES), 1
    )
    bands, weights = [], []
    for w in range(widths):
        width = width_ref[w]
        inside = jnp.logical_and(tap >= 0, tap < width)
        bands.append(jnp.where(inside, 1.0, 0.0).astype(jnp.bfloat16))
        weights.append(1.0 / jnp.sqrt(jnp.full((trials, LANES), width, jnp.int32).astype(F32)))
    band = jnp.concatenate(bands, axis=1)
    lane = lane_iota(trials)
    row_count = owners * periods

    def moved(row, by):
        if by == 0:
            return row
        rolled = [pltpu.roll(block, LANES - by, 1) for block in row]
        out = []
        for b in range(bin_blocks + 1):
            after = rolled[min(b + 1, bin_blocks)]
            out.append(jnp.where(lane < LANES - by, rolled[b], after))
        return out

    for group in range(row_count // GROUP):
        rows = []
        for r in range(GROUP):
            at = (1 + group * GROUP + r) * row_len
            rows.append(
                [
                    rows_in[at + b * trials : at + (b + 1) * trials, :]
                    for b in range(bin_blocks + 1)
                ]
            )
        for level in range(LEVELS):
            half = 2**level
            new = []
            for start in range(0, GROUP, 2 * half):
                for j in range(2 * half):
                    upper = rows[start + j // 2]
                    lower = moved(rows[start + half + j // 2], (j + 1) // 2)
                    new.append([u + low for u, low in zip(upper, lower)])
            rows = new
        for r in range(GROUP):
            row = group * GROUP + r
            for b in range(bin_blocks + 1):
                at = (b * GROUP + r) * trials
                folded[at : at + trials, :] = rows[r][b]
                if b < bin_blocks:
                    first = (row // 8 * bin_blocks + b) * 8 + row % 8
                    step = row_count * bin_blocks
                    ffa_ref[pl.ds(first, trials, stride=step), :] = rows[r][b]
        span = GROUP * trials
        for b in range(bin_blocks):
            left = jnp.concatenate(
                [folded[i * span : (i + 1) * span, :] for i in (b, b + 1)], axis=1
            )
            product = None
            for _ in range(3):
                high = left.astype(jnp.bfloat16)
                left = left - high.astype(F32)
                term = jnp.dot(high, band, preferred_element_type=F32)
                product = term if product is None else product + term
            for r in range(GROUP):
                row = group * GROUP + r
                for w in range(widths):
                    value = product[
                        r * trials : (r + 1) * trials, w * LANES : (w + 1) * LANES
                    ]
                    first = (row * bin_blocks + b) * widths + w
                    step = row_count * bin_blocks * widths
                    box_ref[pl.ds(first, trials, stride=step), :] = value * weights[w]


def fold_and_box(mine, parts, box_width, periods, trials, owners):
    bin_blocks = ROW_BLOCKS // owners
    widths = box_width.shape[0]
    row_count = owners * periods
    row_len = (bin_blocks + 1) * trials
    ffa_rows = trials * row_count * bin_blocks
    vmem = pl.BlockSpec(memory_space=pltpu.VMEM)
    ffa, box = pl.pallas_call(
        functools.partial(fold_kernel, periods, trials, owners, widths),
        in_specs=[pl.BlockSpec(memory_space=pltpu.SMEM)] + [vmem] * owners,
        out_specs=[vmem, vmem],
        out_shape=[
            jax.ShapeDtypeStruct((ffa_rows, LANES), F32),
            jax.ShapeDtypeStruct((ffa_rows * widths, LANES), F32),
        ],
        scratch_shapes=[
            pltpu.VMEM(((row_count + 1) * row_len, LANES), F32),
            pltpu.VMEM((max(owners - 1, 1), (periods + 1) * row_len, LANES), F32),
            pltpu.VMEM((GROUP * row_len, LANES), F32),
        ],
        compiler_params=pltpu.CompilerParams(vmem_limit_bytes=VMEM_LIMIT),
        name="fold",
    )(box_width, mine, *parts)
    bins = bin_blocks * LANES
    ffa = ffa.reshape(trials, row_count // 8, bin_blocks, 8, LANES)
    ffa = ffa.transpose(0, 1, 3, 2, 4).reshape(trials, row_count, bins)
    box = box.reshape(trials, row_count, bin_blocks, widths, LANES)
    box = box.transpose(0, 1, 3, 2, 4).reshape(trials, row_count, widths, bins)
    return ffa, box


def per_device(filterbank, chan_delay, sub_delay, box_width):
    chan_size, owners = lax.axis_size("chan"), lax.axis_size("tm")
    samples = filterbank.shape[1]
    subs, trials = NSUB // chan_size, NDM // chan_size
    blocks, periods = samples // LANES, samples // NBIN
    quad = math.gcd(chan_size, 4)
    own = subband_sums(filterbank, chan_delay, subs)
    parts = [own] + [
        lax.ppermute(own, "chan", pairs(chan_size, flip)) for flip in range(1, quad)
    ]
    sizes = (blocks, subs, trials)
    flips = tuple(range(quad, chan_size, quad))
    far = trial_sums(parts, sub_delay, *sizes, flips, True) if flips else []
    far = [
        lax.ppermute(part, "chan", pairs(chan_size, flip))
        for part, flip in zip(far, flips)
    ]
    (near,) = trial_sums(parts, sub_delay, *sizes, (0,), False)
    mine, *sends = cut_by_phase(near, far, blocks, trials, owners)
    got = [
        lax.ppermute(send, "tm", pairs(owners, flip + 1))
        for flip, send in enumerate(sends)
    ]
    return fold_and_box(mine, got, box_width, periods, trials, owners)


def solution(mesh):
    placed = (P("chan", "tm"), P("chan"), P(), P())
    return jax.shard_map(
        per_device,
        mesh=mesh,
        in_specs=placed,
        out_specs=(P("chan", None, "tm"), P("chan", None, None, "tm")),
        check_vma=False,
    )
```

```python
import functools
import math

import jax
import jax.numpy as jnp
from jax import lax
from jax.experimental import pallas as pl
from jax.experimental.pallas import tpu as pltpu
from jax.sharding import PartitionSpec as P

NCHAN = 4096
NSUB = 64
NDM = 64
NBIN = 2048
LEVELS = 4
MAXW = 32
D1MAX = 128
D2MAX = 896

LANES = 128
F32 = jnp.float32
GROUP = 2**LEVELS
ROW_BLOCKS = NBIN // LANES
LEAD = (D1MAX + D2MAX) // LANES
VMEM_LIMIT = 48 << 20
SCALE = 2.0 ** (-LEVELS / 2) / math.sqrt(NCHAN)


def lane_iota(rows):
    return lax.broadcasted_iota(jnp.int32, (rows, LANES), 1)


def column_exponent(peak):
    return jnp.floor(jnp.log2(jnp.maximum(peak, 2.0**-110))) - 14.0


def scaled(values, exponent):
    return jnp.clip(jnp.round(values * jnp.exp2(-exponent)), -32767.0, 32767.0)


def to_i16(values):
    return values.astype(jnp.int32).astype(jnp.int16)


def pairs(size, flip):
    return [(i, i ^ flip) for i in range(size)]


def subband_kernel(chans, blocks, subs, delay_hbm, x_hbm, out_ref, *scratch):
    delay_ref, x_ref, turned, late, sums, x_sem, delay_sem = scratch
    delay_copy = pltpu.make_async_copy(delay_hbm, delay_ref, delay_sem)
    delay_copy.start()

    def x_copy(sub):
        return pltpu.make_async_copy(
            x_hbm.at[pl.ds(sub * chans, chans), :], x_ref.at[sub], x_sem.at[sub]
        )

    for sub in range(subs):
        x_copy(sub).start()
    delay_copy.wait()
    lane = lane_iota(8)
    tiles = blocks // 8

    @pl.loop(0, subs)
    def _(sub):
        x_copy(sub).wait()
        here = [jnp.zeros((8, LANES), F32)] * tiles
        before = [jnp.zeros((8, LANES), F32)] * tiles
        for octet in range(chans // 8):
            if octet % 2 == 0:
                for block in range(blocks):
                    both = x_ref[
                        sub,
                        8 * octet : 8 * octet + 16,
                        block * LANES : (block + 1) * LANES,
                    ].astype(F32)
                    for k in range(2):
                        at = ((octet + k) * blocks + block) * 8
                        turned[at : at + 8, :] = both[8 * k : 8 * k + 8]
            for i in range(8):
                delay = delay_ref[sub * chans + octet * 8 + i]
                shift = (2 * LANES - delay) & (LANES - 1)
                stays = lane < LANES - delay
                for t in range(tiles):
                    first = (octet * blocks + t * 8) * 8 + i
                    value = turned[pl.ds(first, 8, stride=8), :]
                    value = pltpu.roll(value, shift, 1)
                    here[t] = here[t] + jnp.where(stays, value, 0.0)
                    before[t] = before[t] + jnp.where(stays, 0.0, value)
        for t in range(tiles):
            late[8 * t : 8 * t + 8, :] = before[t]
        late[blocks : blocks + 8, :] = jnp.zeros((8, LANES), F32)
        sums[pl.ds(sub, 1), :] = late[0:1, :]
        for t in range(tiles):
            sums[pl.ds((8 * t + 1) * subs + sub, 8, stride=subs), :] = (
                here[t] + late[8 * t + 1 : 8 * t + 9, :]
            )

    rows = (blocks + 1) * subs
    values = sums[...].reshape(blocks + 1, subs, LANES)
    exponent = column_exponent(jnp.max(jnp.abs(values), axis=0))
    out_ref[0:rows, :] = to_i16(scaled(values, exponent[None]).reshape(rows, LANES))
    out_ref[rows : rows + subs, :] = to_i16(exponent)


def subband_sums(filterbank, chan_delay, subs):
    chans_here, samples = filterbank.shape
    chans, blocks = chans_here // subs, samples // LANES
    rows = (blocks + 2) * subs
    return pl.pallas_call(
        functools.partial(subband_kernel, chans, blocks, subs),
        in_specs=[pl.BlockSpec(memory_space=pltpu.HBM)] * 2,
        out_specs=pl.BlockSpec(memory_space=pltpu.VMEM),
        out_shape=jax.ShapeDtypeStruct((rows, LANES), jnp.int16),
        scratch_shapes=[
            pltpu.SMEM((chans_here,), jnp.int32),
            pltpu.VMEM((subs, chans, samples), filterbank.dtype),
            pltpu.VMEM((chans * blocks, LANES), F32),
            pltpu.VMEM((blocks + 8, LANES), F32),
            pltpu.VMEM(((blocks + 1) * subs, LANES), F32),
            pltpu.SemaphoreType.DMA((subs,)),
            pltpu.SemaphoreType.DMA(()),
        ],
        compiler_params=pltpu.CompilerParams(vmem_limit_bytes=VMEM_LIMIT),
        name="subbands",
    )(chan_delay, filterbank)


def trial_kernel(blocks, subs, trials, origins, flips, primed, coded, delay_ref, *refs):
    refs = list(refs)
    take = lambda n: [refs.pop(0) for _ in range(n)]
    parts = take(len(origins))
    priors = take(len(flips)) if primed else []
    outs = take(len(flips))
    spread, late, acc = refs
    chan = lax.axis_index("chan")
    out_blocks = LEAD + blocks
    depth = out_blocks + LEAD
    for at, part in enumerate(parts):
        base = at * depth * subs
        rows = (blocks + 1) * subs
        scale = jnp.exp2(part[rows : rows + subs, :].astype(F32))
        lead = (LEAD - 1) * subs
        spread[base : base + lead, :] = jnp.zeros((lead, LANES), F32)
        tail = base + lead + rows
        spread[tail : base + depth * subs, :] = jnp.zeros(
            (depth * subs - lead - rows, LANES), F32
        )
        values = part[0:rows, :].astype(F32).reshape(blocks + 1, subs, LANES)
        spread[base + lead : tail, :] = (values * scale[None]).reshape(rows, LANES)

    lane = lane_iota(8)
    tiles = out_blocks // 8

    def one_trial(trial, owner, prior, out):
        here = [jnp.zeros((8, LANES), F32)] * tiles
        before = [jnp.zeros((8, LANES), F32)] * tiles
        for at, origin in enumerate(origins):
            for sub in range(subs):
                delay = delay_ref[owner * trials + trial, (chan ^ origin) * subs + sub]
                shift = delay & (LANES - 1)
                stays = lane < LANES - shift
                back = (LANES - shift) & (LANES - 1)
                for t in range(tiles):
                    first = (at * depth + (delay >> 7) + 8 * t) * subs + sub
                    value = spread[pl.ds(first, 8, stride=subs), :]
                    value = pltpu.roll(value, back, 1)
                    here[t] = here[t] + jnp.where(stays, value, 0.0)
                    before[t] = before[t] + jnp.where(stays, 0.0, value)
        for t in range(tiles):
            late[8 * t : 8 * t + 8, :] = before[t]
        late[out_blocks : out_blocks + 8, :] = jnp.zeros((8, LANES), F32)
        for t in range(tiles):
            rows = pl.ds(8 * t * trials + trial, 8, stride=trials)
            value = here[t] + late[8 * t + 1 : 8 * t + 9, :]
            out[rows, :] = value if prior is None else value + prior[rows, :]

    rows = out_blocks * trials
    for i, (flip, out) in enumerate(zip(flips, outs)):
        target = acc if coded else out

        @pl.loop(0, trials)
        def _(trial):
            one_trial(trial, chan ^ flip, priors[i] if primed else None, target)

        if coded:
            values = acc[...].reshape(out_blocks, trials, LANES)
            exponent = column_exponent(jnp.max(jnp.abs(values), axis=0))
            out[0:rows, :] = to_i16(
                scaled(values, exponent[None]).reshape(rows, LANES)
            )
            out[rows : rows + trials, :] = to_i16(exponent)


def trial_sums(parts, origins, sub_delay, sizes, flips, priors=None, coded=False):
    if not flips:
        return []
    blocks, subs, trials = sizes
    out_blocks = LEAD + blocks
    depth = out_blocks + LEAD
    rows = out_blocks * trials
    out = jax.ShapeDtypeStruct(
        (rows + trials if coded else rows, LANES), jnp.int16 if coded else F32
    )
    vmem = pl.BlockSpec(memory_space=pltpu.VMEM)
    arrays = [*parts, *(priors or [])]
    return pl.pallas_call(
        functools.partial(
            trial_kernel, *sizes, tuple(origins), tuple(flips), bool(priors), coded
        ),
        in_specs=[pl.BlockSpec(memory_space=pltpu.SMEM)] + [vmem] * len(arrays),
        out_specs=[vmem] * len(flips),
        out_shape=[out] * len(flips),
        scratch_shapes=[
            pltpu.VMEM((len(parts) * depth * subs, LANES), F32),
            pltpu.VMEM((out_blocks + 8, LANES), F32),
            pltpu.VMEM((rows, LANES), F32),
        ],
        compiler_params=pltpu.CompilerParams(vmem_limit_bytes=VMEM_LIMIT),
        name="trials_coded" if coded else "trials",
    )(sub_delay, *arrays)


def cut_kernel(blocks, trials, owners, n_far, own_ref, *refs):
    far, mine, sends = refs[:n_far], refs[n_far], refs[n_far + 1 : n_far + owners]
    series, whole, piece = refs[n_far + owners :]
    here = lax.axis_index("tm")
    out_blocks = LEAD + blocks
    rows = out_blocks * trials
    total = own_ref[...].reshape(out_blocks, trials, LANES)
    for part in far:
        scale = jnp.exp2(part[rows : rows + trials, :].astype(F32))
        values = part[0:rows, :].astype(F32).reshape(out_blocks, trials, LANES)
        total = total + values * scale[None]
    total = total * SCALE
    ahead = (ROW_BLOCKS - LEAD) * trials
    exponent = column_exponent(jnp.max(jnp.abs(total), axis=0))
    for target, values in ((series, total), (whole, scaled(total, exponent[None]))):
        target[0:ahead, :] = jnp.zeros((ahead, LANES), F32)
        target[ahead : ahead + rows, :] = values.reshape(rows, LANES)
    periods = blocks // ROW_BLOCKS
    bin_blocks = ROW_BLOCKS // owners
    for flip in range(owners):
        source, target = (series, mine) if flip == 0 else (whole, piece)
        at = 0
        for period in range(periods + 1):
            for j in range(bin_blocks + 1):
                block = ((here ^ flip) * bin_blocks + j) & (ROW_BLOCKS - 1)
                first = (period * ROW_BLOCKS + block) * trials
                target[at : at + trials, :] = source[pl.ds(first, trials), :]
                at += trials
        if flip:
            sends[flip - 1][0:at, :] = to_i16(piece[...])
            sends[flip - 1][at : at + trials, :] = to_i16(exponent)


def cut_by_phase(own, far, blocks, trials, owners):
    out_blocks = LEAD + blocks
    periods = blocks // ROW_BLOCKS
    bin_blocks = ROW_BLOCKS // owners
    rows = (periods + 1) * (bin_blocks + 1) * trials
    vmem = pl.BlockSpec(memory_space=pltpu.VMEM)
    held = (out_blocks + ROW_BLOCKS - LEAD) * trials
    return pl.pallas_call(
        functools.partial(cut_kernel, blocks, trials, owners, len(far)),
        in_specs=[vmem] * (1 + len(far)),
        out_specs=[vmem] * owners,
        out_shape=[jax.ShapeDtypeStruct((rows, LANES), F32)]
        + [jax.ShapeDtypeStruct((rows + trials, LANES), jnp.int16)] * (owners - 1),
        scratch_shapes=[
            pltpu.VMEM((held, LANES), F32),
            pltpu.VMEM((held, LANES), F32),
            pltpu.VMEM((rows, LANES), F32),
        ],
        compiler_params=pltpu.CompilerParams(vmem_limit_bytes=VMEM_LIMIT),
        name="cut",
    )(own, *far)


def fold_kernel(periods, trials, owners, widths, width_ref, mine_ref, *refs):
    parts, (ffa_ref, box_ref) = refs[: owners - 1], refs[owners - 1 : owners + 1]
    rows_in, code, folded = refs[owners + 1 :]
    here = lax.axis_index("tm")
    bin_blocks = ROW_BLOCKS // owners
    row_len = (bin_blocks + 1) * trials
    held = periods * row_len
    rows_in[0:row_len, :] = jnp.zeros((row_len, LANES), F32)
    for flip in range(owners):
        if flip == 0:
            rest = mine_ref[row_len : row_len + held, :]
        else:
            part = parts[flip - 1]
            total = row_len + held
            scale = jnp.exp2(part[total : total + trials, :].astype(F32))
            values = part[0:total, :].astype(F32)
            values = values.reshape(total // trials, trials, LANES) * scale[None]
            code[flip - 1] = values.reshape(total, LANES)
            rest = code[flip - 1, row_len : row_len + held, :]
        first = (here ^ flip) * held + row_len
        rows_in[pl.ds(first, held), :] = rest
    for flip in range(owners):
        early = mine_ref[0:row_len, :] if flip == 0 else code[flip - 1, 0:row_len, :]
        first = (here ^ flip) * held
        rows_in[pl.ds(first, row_len), :] += early

    tap = lax.broadcasted_iota(jnp.int32, (2 * LANES, LANES), 0) - lax.broadcasted_iota(
        jnp.int32, (2 * LANES, LANES), 1
    )
    bands, weights = [], []
    for w in range(widths):
        width = width_ref[w]
        inside = jnp.logical_and(tap >= 0, tap < width)
        bands.append(jnp.where(inside, 1.0, 0.0).astype(jnp.bfloat16))
        weights.append(1.0 / jnp.sqrt(jnp.full((trials, LANES), width, jnp.int32).astype(F32)))
    band = jnp.concatenate(bands, axis=1)
    lane = lane_iota(trials)
    row_count = owners * periods

    def moved(row, by):
        if by == 0:
            return row
        rolled = [pltpu.roll(block, LANES - by, 1) for block in row]
        out = []
        for b in range(bin_blocks + 1):
            after = rolled[min(b + 1, bin_blocks)]
            out.append(jnp.where(lane < LANES - by, rolled[b], after))
        return out

    for group in range(row_count // GROUP):
        rows = []
        for r in range(GROUP):
            at = (1 + group * GROUP + r) * row_len
            rows.append(
                [
                    rows_in[at + b * trials : at + (b + 1) * trials, :]
                    for b in range(bin_blocks + 1)
                ]
            )
        for level in range(LEVELS):
            half = 2**level
            new = []
            for start in range(0, GROUP, 2 * half):
                for j in range(2 * half):
                    upper = rows[start + j // 2]
                    lower = moved(rows[start + half + j // 2], (j + 1) // 2)
                    new.append([u + low for u, low in zip(upper, lower)])
            rows = new
        for r in range(GROUP):
            row = group * GROUP + r
            for b in range(bin_blocks + 1):
                at = (b * GROUP + r) * trials
                folded[at : at + trials, :] = rows[r][b]
                if b < bin_blocks:
                    first = (row // 8 * bin_blocks + b) * 8 + row % 8
                    step = row_count * bin_blocks
                    ffa_ref[pl.ds(first, trials, stride=step), :] = rows[r][b]
        span = GROUP * trials
        for b in range(bin_blocks):
            left = jnp.concatenate(
                [folded[i * span : (i + 1) * span, :] for i in (b, b + 1)], axis=1
            )
            product = None
            for _ in range(3):
                high = left.astype(jnp.bfloat16)
                left = left - high.astype(F32)
                term = jnp.dot(high, band, preferred_element_type=F32)
                product = term if product is None else product + term
            for r in range(GROUP):
                row = group * GROUP + r
                for w in range(widths):
                    value = product[
                        r * trials : (r + 1) * trials, w * LANES : (w + 1) * LANES
                    ]
                    first = (row * bin_blocks + b) * widths + w
                    step = row_count * bin_blocks * widths
                    box_ref[pl.ds(first, trials, stride=step), :] = value * weights[w]


def fold_and_box(mine, parts, box_width, periods, trials, owners):
    bin_blocks = ROW_BLOCKS // owners
    widths = box_width.shape[0]
    row_count = owners * periods
    row_len = (bin_blocks + 1) * trials
    ffa_rows = trials * row_count * bin_blocks
    vmem = pl.BlockSpec(memory_space=pltpu.VMEM)
    ffa, box = pl.pallas_call(
        functools.partial(fold_kernel, periods, trials, owners, widths),
        in_specs=[pl.BlockSpec(memory_space=pltpu.SMEM)] + [vmem] * owners,
        out_specs=[vmem, vmem],
        out_shape=[
            jax.ShapeDtypeStruct((ffa_rows, LANES), F32),
            jax.ShapeDtypeStruct((ffa_rows * widths, LANES), F32),
        ],
        scratch_shapes=[
            pltpu.VMEM(((row_count + 1) * row_len, LANES), F32),
            pltpu.VMEM((max(owners - 1, 1), (periods + 1) * row_len, LANES), F32),
            pltpu.VMEM((GROUP * row_len, LANES), F32),
        ],
        compiler_params=pltpu.CompilerParams(vmem_limit_bytes=VMEM_LIMIT),
        name="fold",
    )(box_width, mine, *parts)
    bins = bin_blocks * LANES
    ffa = ffa.reshape(trials, row_count // 8, bin_blocks, 8, LANES)
    ffa = ffa.transpose(0, 1, 3, 2, 4).reshape(trials, row_count, bins)
    box = box.reshape(trials, row_count, bin_blocks, widths, LANES)
    box = box.transpose(0, 1, 3, 2, 4).reshape(trials, row_count, widths, bins)
    return ffa, box


def per_device(filterbank, chan_delay, sub_delay, box_width):
    chan_size, owners = lax.axis_size("chan"), lax.axis_size("tm")
    samples = filterbank.shape[1]
    subs, trials = NSUB // chan_size, NDM // chan_size
    blocks, periods = samples // LANES, samples // NBIN
    quad = math.gcd(chan_size, 4)
    own = subband_sums(filterbank, chan_delay, subs)
    part = {0: own}
    for flip in range(1, quad):
        part[flip] = lax.ppermute(own, "chan", pairs(chan_size, flip))
    sizes = (blocks, subs, trials)
    flips = tuple(range(quad, chan_size, quad))
    sums = trial_sums([own], (0,), sub_delay, sizes, (*flips, 0))
    rest = tuple(range(1, quad))
    if quad == 4:
        sums = trial_sums([part[2]], (2,), sub_delay, sizes, (*flips, 0), sums)
        rest = (1, 3)
    last = [part[flip] for flip in rest]
    far = trial_sums(last, rest, sub_delay, sizes, flips, sums[:-1], True)
    far = [
        lax.ppermute(send, "chan", pairs(chan_size, flip))
        for send, flip in zip(far, flips)
    ]
    (near,) = trial_sums(last, rest, sub_delay, sizes, (0,), sums[-1:])
    mine, *sends = cut_by_phase(near, far, blocks, trials, owners)
    got = [
        lax.ppermute(send, "tm", pairs(owners, flip + 1))
        for flip, send in enumerate(sends)
    ]
    return fold_and_box(mine, got, box_width, periods, trials, owners)


def solution(mesh):
    placed = (P("chan", "tm"), P("chan"), P(), P())
    return jax.shard_map(
        per_device,
        mesh=mesh,
        in_specs=placed,
        out_specs=(P("chan", None, "tm"), P("chan", None, None, "tm")),
        check_vma=False,
    )
```

```python
import functools
import math

import jax
import jax.numpy as jnp
from jax import lax
from jax.experimental import pallas as pl
from jax.experimental.pallas import tpu as pltpu
from jax.sharding import PartitionSpec as P

NCHAN = 4096
NSUB = 64
NDM = 64
NBIN = 2048
LEVELS = 4
MAXW = 32
D1MAX = 128
D2MAX = 896

LANES = 128
F32 = jnp.float32
GROUP = 2**LEVELS
ROW_BLOCKS = NBIN // LANES
LEAD = (D1MAX + D2MAX) // LANES
VMEM_LIMIT = 48 << 20
SCALE = 2.0 ** (-LEVELS / 2) / math.sqrt(NCHAN)


def lane_iota(rows):
    return lax.broadcasted_iota(jnp.int32, (rows, LANES), 1)


def column_exponent(peak):
    return jnp.floor(jnp.log2(jnp.maximum(peak, 2.0**-110))) - 14.0


def scaled(values, exponent):
    return jnp.clip(jnp.round(values * jnp.exp2(-exponent)), -32767.0, 32767.0)


def to_i16(values):
    return values.astype(jnp.int32).astype(jnp.int16)


def pairs(size, flip):
    return [(i, i ^ flip) for i in range(size)]


def subband_kernel(chans, blocks, subs, delay_hbm, x_hbm, out_ref, *scratch):
    delay_ref, x_ref, turned, late, sums, x_sem, delay_sem = scratch
    delay_copy = pltpu.make_async_copy(delay_hbm, delay_ref, delay_sem)
    delay_copy.start()

    def x_copy(sub):
        return pltpu.make_async_copy(
            x_hbm.at[pl.ds(sub * chans, chans), :], x_ref.at[sub], x_sem.at[sub]
        )

    for sub in range(subs):
        x_copy(sub).start()
    delay_copy.wait()
    lane = lane_iota(8)
    tiles = blocks // 8

    @pl.loop(0, subs)
    def _(sub):
        x_copy(sub).wait()
        here = [jnp.zeros((8, LANES), F32)] * tiles
        before = [jnp.zeros((8, LANES), F32)] * tiles
        for octet in range(chans // 8):
            if octet % 2 == 0:
                for block in range(blocks):
                    both = x_ref[
                        sub,
                        8 * octet : 8 * octet + 16,
                        block * LANES : (block + 1) * LANES,
                    ].astype(F32)
                    for k in range(2):
                        at = ((octet + k) * blocks + block) * 8
                        turned[at : at + 8, :] = both[8 * k : 8 * k + 8]
            for i in range(8):
                delay = delay_ref[sub * chans + octet * 8 + i]
                shift = (2 * LANES - delay) & (LANES - 1)
                stays = lane < LANES - delay
                for t in range(tiles):
                    first = (octet * blocks + t * 8) * 8 + i
                    value = turned[pl.ds(first, 8, stride=8), :]
                    value = pltpu.roll(value, shift, 1)
                    here[t] = here[t] + jnp.where(stays, value, 0.0)
                    before[t] = before[t] + jnp.where(stays, 0.0, value)
        for t in range(tiles):
            late[8 * t : 8 * t + 8, :] = before[t]
        late[blocks : blocks + 8, :] = jnp.zeros((8, LANES), F32)
        sums[pl.ds(sub, 1), :] = late[0:1, :]
        for t in range(tiles):
            sums[pl.ds((8 * t + 1) * subs + sub, 8, stride=subs), :] = (
                here[t] + late[8 * t + 1 : 8 * t + 9, :]
            )

    rows = (blocks + 1) * subs
    values = sums[...].reshape(blocks + 1, subs, LANES)
    exponent = column_exponent(jnp.max(jnp.abs(values), axis=0))
    out_ref[0:rows, :] = to_i16(scaled(values, exponent[None]).reshape(rows, LANES))
    out_ref[rows : rows + subs, :] = to_i16(exponent)


def subband_sums(filterbank, chan_delay, subs):
    chans_here, samples = filterbank.shape
    chans, blocks = chans_here // subs, samples // LANES
    rows = (blocks + 2) * subs
    return pl.pallas_call(
        functools.partial(subband_kernel, chans, blocks, subs),
        in_specs=[pl.BlockSpec(memory_space=pltpu.HBM)] * 2,
        out_specs=pl.BlockSpec(memory_space=pltpu.VMEM),
        out_shape=jax.ShapeDtypeStruct((rows, LANES), jnp.int16),
        scratch_shapes=[
            pltpu.SMEM((chans_here,), jnp.int32),
            pltpu.VMEM((subs, chans, samples), filterbank.dtype),
            pltpu.VMEM((chans * blocks, LANES), F32),
            pltpu.VMEM((blocks + 8, LANES), F32),
            pltpu.VMEM(((blocks + 1) * subs, LANES), F32),
            pltpu.SemaphoreType.DMA((subs,)),
            pltpu.SemaphoreType.DMA(()),
        ],
        compiler_params=pltpu.CompilerParams(vmem_limit_bytes=VMEM_LIMIT),
        name="subbands",
    )(pltpu.with_memory_space_constraint(chan_delay, pltpu.HBM), filterbank)


def trial_kernel(blocks, subs, trials, origins, flips, primed, coded, delay_ref, *refs):
    refs = list(refs)
    take = lambda n: [refs.pop(0) for _ in range(n)]
    parts = take(len(origins))
    priors = take(len(flips)) if primed else []
    outs = take(len(flips))
    spread, late, acc = refs
    chan = lax.axis_index("chan")
    out_blocks = LEAD + blocks
    depth = out_blocks + LEAD
    for at, part in enumerate(parts):
        base = at * depth * subs
        rows = (blocks + 1) * subs
        scale = jnp.exp2(part[rows : rows + subs, :].astype(F32))
        lead = (LEAD - 1) * subs
        spread[base : base + lead, :] = jnp.zeros((lead, LANES), F32)
        tail = base + lead + rows
        spread[tail : base + depth * subs, :] = jnp.zeros(
            (depth * subs - lead - rows, LANES), F32
        )
        values = part[0:rows, :].astype(F32).reshape(blocks + 1, subs, LANES)
        spread[base + lead : tail, :] = (values * scale[None]).reshape(rows, LANES)

    lane = lane_iota(8)
    tiles = out_blocks // 8

    def one_trial(trial, owner, prior, out):
        here = [jnp.zeros((8, LANES), F32)] * tiles
        before = [jnp.zeros((8, LANES), F32)] * tiles
        for at, origin in enumerate(origins):
            for sub in range(subs):
                delay = delay_ref[owner * trials + trial, (chan ^ origin) * subs + sub]
                shift = delay & (LANES - 1)
                stays = lane < LANES - shift
                back = (LANES - shift) & (LANES - 1)
                for t in range(tiles):
                    first = (at * depth + (delay >> 7) + 8 * t) * subs + sub
                    value = spread[pl.ds(first, 8, stride=subs), :]
                    value = pltpu.roll(value, back, 1)
                    here[t] = here[t] + jnp.where(stays, value, 0.0)
                    before[t] = before[t] + jnp.where(stays, 0.0, value)
        for t in range(tiles):
            late[8 * t : 8 * t + 8, :] = before[t]
        late[out_blocks : out_blocks + 8, :] = jnp.zeros((8, LANES), F32)
        for t in range(tiles):
            rows = pl.ds(8 * t * trials + trial, 8, stride=trials)
            value = here[t] + late[8 * t + 1 : 8 * t + 9, :]
            out[rows, :] = value if prior is None else value + prior[rows, :]

    rows = out_blocks * trials
    for i, (flip, out) in enumerate(zip(flips, outs)):
        target = acc if coded else out

        @pl.loop(0, trials, unroll=trials)
        def _(trial):
            one_trial(trial, chan ^ flip, priors[i] if primed else None, target)

        if coded:
            values = acc[...].reshape(out_blocks, trials, LANES)
            exponent = column_exponent(jnp.max(jnp.abs(values), axis=0))
            out[0:rows, :] = to_i16(
                scaled(values, exponent[None]).reshape(rows, LANES)
            )
            out[rows : rows + trials, :] = to_i16(exponent)


def trial_sums(parts, origins, sub_delay, sizes, flips, priors=None, coded=False):
    if not flips:
        return []
    blocks, subs, trials = sizes
    out_blocks = LEAD + blocks
    depth = out_blocks + LEAD
    rows = out_blocks * trials
    out = jax.ShapeDtypeStruct(
        (rows + trials if coded else rows, LANES), jnp.int16 if coded else F32
    )
    vmem = pl.BlockSpec(memory_space=pltpu.VMEM)
    arrays = [*parts, *(priors or [])]
    return pl.pallas_call(
        functools.partial(
            trial_kernel, *sizes, tuple(origins), tuple(flips), bool(priors), coded
        ),
        in_specs=[pl.BlockSpec(memory_space=pltpu.SMEM)] + [vmem] * len(arrays),
        out_specs=[vmem] * len(flips),
        out_shape=[out] * len(flips),
        scratch_shapes=[
            pltpu.VMEM((len(parts) * depth * subs, LANES), F32),
            pltpu.VMEM((out_blocks + 8, LANES), F32),
            pltpu.VMEM((rows, LANES), F32),
        ],
        compiler_params=pltpu.CompilerParams(vmem_limit_bytes=VMEM_LIMIT),
        name="trials_coded" if coded else "trials",
    )(sub_delay, *arrays)


def cut_kernel(blocks, trials, owners, n_far, own_ref, *refs):
    far, mine, sends = refs[:n_far], refs[n_far], refs[n_far + 1 : n_far + owners]
    series, whole, piece = refs[n_far + owners :]
    here = lax.axis_index("tm")
    out_blocks = LEAD + blocks
    rows = out_blocks * trials
    total = own_ref[...].reshape(out_blocks, trials, LANES)
    for part in far:
        scale = jnp.exp2(part[rows : rows + trials, :].astype(F32))
        values = part[0:rows, :].astype(F32).reshape(out_blocks, trials, LANES)
        total = total + values * scale[None]
    total = total * SCALE
    ahead = (ROW_BLOCKS - LEAD) * trials
    exponent = column_exponent(jnp.max(jnp.abs(total), axis=0))
    for target, values in ((series, total), (whole, scaled(total, exponent[None]))):
        target[0:ahead, :] = jnp.zeros((ahead, LANES), F32)
        target[ahead : ahead + rows, :] = values.reshape(rows, LANES)
    periods = blocks // ROW_BLOCKS
    bin_blocks = ROW_BLOCKS // owners
    for flip in range(owners):
        source, target = (series, mine) if flip == 0 else (whole, piece)
        at = 0
        for period in range(periods + 1):
            for j in range(bin_blocks + 1):
                block = ((here ^ flip) * bin_blocks + j) & (ROW_BLOCKS - 1)
                first = (period * ROW_BLOCKS + block) * trials
                target[at : at + trials, :] = source[pl.ds(first, trials), :]
                at += trials
        if flip:
            sends[flip - 1][0:at, :] = to_i16(piece[...])
            sends[flip - 1][at : at + trials, :] = to_i16(exponent)


def cut_by_phase(own, far, blocks, trials, owners):
    out_blocks = LEAD + blocks
    periods = blocks // ROW_BLOCKS
    bin_blocks = ROW_BLOCKS // owners
    rows = (periods + 1) * (bin_blocks + 1) * trials
    vmem = pl.BlockSpec(memory_space=pltpu.VMEM)
    held = (out_blocks + ROW_BLOCKS - LEAD) * trials
    return pl.pallas_call(
        functools.partial(cut_kernel, blocks, trials, owners, len(far)),
        in_specs=[vmem] * (1 + len(far)),
        out_specs=[vmem] * owners,
        out_shape=[jax.ShapeDtypeStruct((rows, LANES), F32)]
        + [jax.ShapeDtypeStruct((rows + trials, LANES), jnp.int16)] * (owners - 1),
        scratch_shapes=[
            pltpu.VMEM((held, LANES), F32),
            pltpu.VMEM((held, LANES), F32),
            pltpu.VMEM((rows, LANES), F32),
        ],
        compiler_params=pltpu.CompilerParams(vmem_limit_bytes=VMEM_LIMIT),
        name="cut",
    )(own, *far)


def fold_kernel(periods, trials, owners, widths, width_ref, mine_ref, *refs):
    parts, (ffa_ref, box_ref) = refs[: owners - 1], refs[owners - 1 : owners + 1]
    rows_in, code, folded = refs[owners + 1 :]
    here = lax.axis_index("tm")
    bin_blocks = ROW_BLOCKS // owners
    row_len = (bin_blocks + 1) * trials
    held = periods * row_len
    rows_in[0:row_len, :] = jnp.zeros((row_len, LANES), F32)
    for flip in range(owners):
        if flip == 0:
            rest = mine_ref[row_len : row_len + held, :]
        else:
            part = parts[flip - 1]
            total = row_len + held
            scale = jnp.exp2(part[total : total + trials, :].astype(F32))
            values = part[0:total, :].astype(F32)
            values = values.reshape(total // trials, trials, LANES) * scale[None]
            code[flip - 1] = values.reshape(total, LANES)
            rest = code[flip - 1, row_len : row_len + held, :]
        first = (here ^ flip) * held + row_len
        rows_in[pl.ds(first, held), :] = rest
    for flip in range(owners):
        early = mine_ref[0:row_len, :] if flip == 0 else code[flip - 1, 0:row_len, :]
        first = (here ^ flip) * held
        rows_in[pl.ds(first, row_len), :] += early

    tap = lax.broadcasted_iota(jnp.int32, (2 * LANES, LANES), 0) - lax.broadcasted_iota(
        jnp.int32, (2 * LANES, LANES), 1
    )
    bands, weights = [], []
    for w in range(widths):
        width = width_ref[w]
        inside = jnp.logical_and(tap >= 0, tap < width)
        bands.append(jnp.where(inside, 1.0, 0.0).astype(jnp.bfloat16))
        weights.append(1.0 / jnp.sqrt(jnp.full((trials, LANES), width, jnp.int32).astype(F32)))
    band = jnp.concatenate(bands, axis=1)
    lane = lane_iota(trials)
    row_count = owners * periods

    def moved(row, by):
        if by == 0:
            return row
        rolled = [pltpu.roll(block, LANES - by, 1) for block in row]
        out = []
        for b in range(bin_blocks + 1):
            after = rolled[min(b + 1, bin_blocks)]
            out.append(jnp.where(lane < LANES - by, rolled[b], after))
        return out

    for group in range(row_count // GROUP):
        rows = []
        for r in range(GROUP):
            at = (1 + group * GROUP + r) * row_len
            rows.append(
                [
                    rows_in[at + b * trials : at + (b + 1) * trials, :]
                    for b in range(bin_blocks + 1)
                ]
            )
        for level in range(LEVELS):
            half = 2**level
            new = []
            for start in range(0, GROUP, 2 * half):
                for j in range(2 * half):
                    upper = rows[start + j // 2]
                    lower = moved(rows[start + half + j // 2], (j + 1) // 2)
                    new.append([u + low for u, low in zip(upper, lower)])
            rows = new
        for r in range(GROUP):
            row = group * GROUP + r
            for b in range(bin_blocks + 1):
                at = (b * GROUP + r) * trials
                folded[at : at + trials, :] = rows[r][b]
                if b < bin_blocks:
                    first = (row // 8 * bin_blocks + b) * 8 + row % 8
                    step = row_count * bin_blocks
                    ffa_ref[pl.ds(first, trials, stride=step), :] = rows[r][b]
        span = GROUP * trials
        for b in range(bin_blocks):
            left = jnp.concatenate(
                [folded[i * span : (i + 1) * span, :] for i in (b, b + 1)], axis=1
            )
            product = None
            for _ in range(3):
                high = left.astype(jnp.bfloat16)
                left = left - high.astype(F32)
                term = jnp.dot(high, band, preferred_element_type=F32)
                product = term if product is None else product + term
            for r in range(GROUP):
                row = group * GROUP + r
                for w in range(widths):
                    value = product[
                        r * trials : (r + 1) * trials, w * LANES : (w + 1) * LANES
                    ]
                    first = (row * bin_blocks + b) * widths + w
                    step = row_count * bin_blocks * widths
                    box_ref[pl.ds(first, trials, stride=step), :] = value * weights[w]


def fold_and_box(mine, parts, box_width, periods, trials, owners):
    bin_blocks = ROW_BLOCKS // owners
    widths = box_width.shape[0]
    row_count = owners * periods
    row_len = (bin_blocks + 1) * trials
    ffa_rows = trials * row_count * bin_blocks
    vmem = pl.BlockSpec(memory_space=pltpu.VMEM)
    ffa, box = pl.pallas_call(
        functools.partial(fold_kernel, periods, trials, owners, widths),
        in_specs=[pl.BlockSpec(memory_space=pltpu.SMEM)] + [vmem] * owners,
        out_specs=[vmem, vmem],
        out_shape=[
            jax.ShapeDtypeStruct((ffa_rows, LANES), F32),
            jax.ShapeDtypeStruct((ffa_rows * widths, LANES), F32),
        ],
        scratch_shapes=[
            pltpu.VMEM(((row_count + 1) * row_len, LANES), F32),
            pltpu.VMEM((max(owners - 1, 1), (periods + 1) * row_len, LANES), F32),
            pltpu.VMEM((GROUP * row_len, LANES), F32),
        ],
        compiler_params=pltpu.CompilerParams(vmem_limit_bytes=VMEM_LIMIT),
        name="fold",
    )(box_width, mine, *parts)
    bins = bin_blocks * LANES
    ffa = ffa.reshape(trials, row_count // 8, bin_blocks, 8, LANES)
    ffa = ffa.transpose(0, 1, 3, 2, 4).reshape(trials, row_count, bins)
    box = box.reshape(trials, row_count, bin_blocks, widths, LANES)
    box = box.transpose(0, 1, 3, 2, 4).reshape(trials, row_count, widths, bins)
    return ffa, box


def per_device(filterbank, chan_delay, sub_delay, box_width):
    chan_size, owners = lax.axis_size("chan"), lax.axis_size("tm")
    samples = filterbank.shape[1]
    subs, trials = NSUB // chan_size, NDM // chan_size
    blocks, periods = samples // LANES, samples // NBIN
    quad = math.gcd(chan_size, 4)
    own = subband_sums(filterbank, chan_delay, subs)
    part = {0: own}
    for flip in range(1, quad):
        part[flip] = lax.ppermute(own, "chan", pairs(chan_size, flip))
    sizes = (blocks, subs, trials)
    flips = tuple(range(quad, chan_size, quad))
    order = [0, 2, 1, 3] if quad == 4 else list(range(quad))
    *early, final = order
    far, near = None, None
    for origin in early:
        both = origin == 0
        sums = trial_sums(
            [part[origin]], (origin,), sub_delay, sizes, (*flips, 0) if both else flips, far
        )
        far, near = (sums[:-1], sums[-1:]) if both else (sums, near)
    far = trial_sums([part[final]], (final,), sub_delay, sizes, flips, far, True)
    far = [
        lax.ppermute(send, "chan", pairs(chan_size, flip))
        for send, flip in zip(far, flips)
    ]
    rest = tuple(order[1:])
    (near,) = trial_sums([part[o] for o in rest], rest, sub_delay, sizes, (0,), near)
    mine, *sends = cut_by_phase(near, far, blocks, trials, owners)
    got = [
        lax.ppermute(send, "tm", pairs(owners, flip + 1))
        for flip, send in enumerate(sends)
    ]
    return fold_and_box(mine, got, box_width, periods, trials, owners)


def solution(mesh):
    placed = (P("chan", "tm"), P("chan"), P(), P())
    return jax.shard_map(
        per_device,
        mesh=mesh,
        in_specs=placed,
        out_specs=(P("chan", None, "tm"), P("chan", None, None, "tm")),
        check_vma=False,
    )
```

```python
import functools
import math

import jax
import jax.numpy as jnp
from jax import lax
from jax.experimental import pallas as pl
from jax.experimental.pallas import tpu as pltpu
from jax.sharding import PartitionSpec as P

NCHAN = 4096
NSUB = 64
NDM = 64
NBIN = 2048
LEVELS = 4
MAXW = 32
D1MAX = 128
D2MAX = 896

LANES = 128
F32 = jnp.float32
GROUP = 2**LEVELS
ROW_BLOCKS = NBIN // LANES
LEAD = (D1MAX + D2MAX) // LANES
VMEM_LIMIT = 48 << 20
SCALE = 2.0 ** (-LEVELS / 2) / math.sqrt(NCHAN)


def lane_iota(rows):
    return lax.broadcasted_iota(jnp.int32, (rows, LANES), 1)


def column_exponent(peak):
    return jnp.floor(jnp.log2(jnp.maximum(peak, 2.0**-110))) - 14.0


def scaled(values, exponent):
    return jnp.clip(jnp.round(values * jnp.exp2(-exponent)), -32767.0, 32767.0)


def to_i16(values):
    return values.astype(jnp.int32).astype(jnp.int16)


def pairs(size, flip):
    return [(i, i ^ flip) for i in range(size)]


def subband_kernel(chans, blocks, subs, delay_hbm, x_hbm, out_ref, *scratch):
    delay_ref, x_ref, turned, late, sums, x_sem, delay_sem = scratch
    delay_copy = pltpu.make_async_copy(delay_hbm, delay_ref, delay_sem)
    delay_copy.start()

    def x_copy(sub):
        return pltpu.make_async_copy(
            x_hbm.at[pl.ds(sub * chans, chans), :], x_ref.at[sub], x_sem.at[sub]
        )

    for sub in range(subs):
        x_copy(sub).start()
    delay_copy.wait()
    lane = lane_iota(8)
    tiles = blocks // 8

    @pl.loop(0, subs)
    def _(sub):
        x_copy(sub).wait()
        here = [jnp.zeros((8, LANES), F32)] * tiles
        before = [jnp.zeros((8, LANES), F32)] * tiles
        for octet in range(chans // 8):
            if octet % 2 == 0:
                for block in range(blocks):
                    both = x_ref[
                        sub,
                        8 * octet : 8 * octet + 16,
                        block * LANES : (block + 1) * LANES,
                    ].astype(F32)
                    for k in range(2):
                        at = ((octet + k) * blocks + block) * 8
                        turned[at : at + 8, :] = both[8 * k : 8 * k + 8]
            for i in range(8):
                delay = delay_ref[sub * chans + octet * 8 + i]
                shift = (2 * LANES - delay) & (LANES - 1)
                stays = lane < LANES - delay
                for t in range(tiles):
                    first = (octet * blocks + t * 8) * 8 + i
                    value = turned[pl.ds(first, 8, stride=8), :]
                    value = pltpu.roll(value, shift, 1)
                    here[t] = here[t] + jnp.where(stays, value, 0.0)
                    before[t] = before[t] + jnp.where(stays, 0.0, value)
        for t in range(tiles):
            late[8 * t : 8 * t + 8, :] = before[t]
        late[blocks : blocks + 8, :] = jnp.zeros((8, LANES), F32)
        sums[pl.ds(sub, 1), :] = late[0:1, :]
        for t in range(tiles):
            sums[pl.ds((8 * t + 1) * subs + sub, 8, stride=subs), :] = (
                here[t] + late[8 * t + 1 : 8 * t + 9, :]
            )

    rows = (blocks + 1) * subs
    values = sums[...].reshape(blocks + 1, subs, LANES)
    exponent = column_exponent(jnp.max(jnp.abs(values), axis=0))
    out_ref[0:rows, :] = to_i16(scaled(values, exponent[None]).reshape(rows, LANES))
    out_ref[rows : rows + subs, :] = to_i16(exponent)


def subband_sums(filterbank, chan_delay, subs):
    chans_here, samples = filterbank.shape
    chans, blocks = chans_here // subs, samples // LANES
    rows = (blocks + 2) * subs
    return pl.pallas_call(
        functools.partial(subband_kernel, chans, blocks, subs),
        in_specs=[pl.BlockSpec(memory_space=pltpu.HBM)] * 2,
        out_specs=pl.BlockSpec(memory_space=pltpu.VMEM),
        out_shape=jax.ShapeDtypeStruct((rows, LANES), jnp.int16),
        scratch_shapes=[
            pltpu.SMEM((chans_here,), jnp.int32),
            pltpu.VMEM((subs, chans, samples), filterbank.dtype),
            pltpu.VMEM((chans * blocks, LANES), F32),
            pltpu.VMEM((blocks + 8, LANES), F32),
            pltpu.VMEM(((blocks + 1) * subs, LANES), F32),
            pltpu.SemaphoreType.DMA((subs,)),
            pltpu.SemaphoreType.DMA(()),
        ],
        compiler_params=pltpu.CompilerParams(vmem_limit_bytes=VMEM_LIMIT),
        name="subbands",
    )(pltpu.with_memory_space_constraint(chan_delay, pltpu.HBM), filterbank)


def trial_kernel(blocks, subs, trials, origins, flips, primed, coded, delays, *refs):
    refs = list(refs)
    take = lambda n: [refs.pop(0) for _ in range(n)]
    parts = take(len(origins))
    priors = take(len(flips)) if primed else []
    outs = take(len(flips))
    spread, late, acc, delay_ref, delay_sem = refs
    chan = lax.axis_index("chan")
    fetched = delay_ref.shape[1]
    copies, offset = [], []
    for i, flip in enumerate(flips):
        wanted = (chan ^ flip) * trials
        first = wanted // fetched * fetched
        offset.append(wanted - first)
        copies.append(
            pltpu.make_async_copy(
                delays.at[pl.ds(pl.multiple_of(first, 8), fetched), :],
                delay_ref.at[i],
                delay_sem.at[i],
            )
        )
        copies[i].start()
    out_blocks = LEAD + blocks
    depth = out_blocks + LEAD
    for at, part in enumerate(parts):
        base = at * depth * subs
        rows = (blocks + 1) * subs
        scale = jnp.exp2(part[rows : rows + subs, :].astype(F32))
        lead = (LEAD - 1) * subs
        spread[base : base + lead, :] = jnp.zeros((lead, LANES), F32)
        tail = base + lead + rows
        spread[tail : base + depth * subs, :] = jnp.zeros(
            (depth * subs - lead - rows, LANES), F32
        )
        values = part[0:rows, :].astype(F32).reshape(blocks + 1, subs, LANES)
        spread[base + lead : tail, :] = (values * scale[None]).reshape(rows, LANES)

    lane = lane_iota(8)
    tiles = out_blocks // 8

    for copy in copies:
        copy.wait()

    def one_trial(trial, i, prior, out):
        here = [jnp.zeros((8, LANES), F32)] * tiles
        before = [jnp.zeros((8, LANES), F32)] * tiles
        for at, origin in enumerate(origins):
            for sub in range(subs):
                delay = delay_ref[i, offset[i] + trial, (chan ^ origin) * subs + sub]
                shift = delay & (LANES - 1)
                stays = lane < LANES - shift
                back = (LANES - shift) & (LANES - 1)
                for t in range(tiles):
                    first = (at * depth + (delay >> 7) + 8 * t) * subs + sub
                    value = spread[pl.ds(first, 8, stride=subs), :]
                    value = pltpu.roll(value, back, 1)
                    here[t] = here[t] + jnp.where(stays, value, 0.0)
                    before[t] = before[t] + jnp.where(stays, 0.0, value)
        for t in range(tiles):
            late[8 * t : 8 * t + 8, :] = before[t]
        late[out_blocks : out_blocks + 8, :] = jnp.zeros((8, LANES), F32)
        for t in range(tiles):
            rows = pl.ds(8 * t * trials + trial, 8, stride=trials)
            value = here[t] + late[8 * t + 1 : 8 * t + 9, :]
            out[rows, :] = value if prior is None else value + prior[rows, :]

    rows = out_blocks * trials
    for i, (flip, out) in enumerate(zip(flips, outs)):
        target = acc if coded else out

        @pl.loop(0, trials, unroll=trials)
        def _(trial):
            one_trial(trial, i, priors[i] if primed else None, target)

        if coded:
            values = acc[...].reshape(out_blocks, trials, LANES)
            exponent = column_exponent(jnp.max(jnp.abs(values), axis=0))
            out[0:rows, :] = to_i16(
                scaled(values, exponent[None]).reshape(rows, LANES)
            )
            out[rows : rows + trials, :] = to_i16(exponent)


def trial_sums(parts, origins, sub_delay, sizes, flips, priors=None, coded=False):
    if not flips:
        return []
    blocks, subs, trials = sizes
    out_blocks = LEAD + blocks
    depth = out_blocks + LEAD
    rows = out_blocks * trials
    out = jax.ShapeDtypeStruct(
        (rows + trials if coded else rows, LANES), jnp.int16 if coded else F32
    )
    vmem = pl.BlockSpec(memory_space=pltpu.VMEM)
    arrays = [*parts, *(priors or [])]
    return pl.pallas_call(
        functools.partial(
            trial_kernel, *sizes, tuple(origins), tuple(flips), bool(priors), coded
        ),
        in_specs=[pl.BlockSpec(memory_space=pl.ANY)] + [vmem] * len(arrays),
        out_specs=[vmem] * len(flips),
        out_shape=[out] * len(flips),
        scratch_shapes=[
            pltpu.VMEM((len(parts) * depth * subs, LANES), F32),
            pltpu.VMEM((out_blocks + 8, LANES), F32),
            pltpu.VMEM((rows, LANES), F32),
            pltpu.SMEM((len(flips), max(trials, 8), sub_delay.shape[1]), jnp.int32),
            pltpu.SemaphoreType.DMA((len(flips),)),
        ],
        compiler_params=pltpu.CompilerParams(vmem_limit_bytes=VMEM_LIMIT),
        name="trials_coded" if coded else "trials",
    )(sub_delay, *arrays)


def cut_kernel(blocks, trials, owners, n_far, own_ref, *refs):
    far, mine, sends = refs[:n_far], refs[n_far], refs[n_far + 1 : n_far + owners]
    series, whole, piece = refs[n_far + owners :]
    here = lax.axis_index("tm")
    out_blocks = LEAD + blocks
    rows = out_blocks * trials
    total = own_ref[...].reshape(out_blocks, trials, LANES)
    for part in far:
        scale = jnp.exp2(part[rows : rows + trials, :].astype(F32))
        values = part[0:rows, :].astype(F32).reshape(out_blocks, trials, LANES)
        total = total + values * scale[None]
    total = total * SCALE
    ahead = (ROW_BLOCKS - LEAD) * trials
    exponent = column_exponent(jnp.max(jnp.abs(total), axis=0))
    for target, values in ((series, total), (whole, scaled(total, exponent[None]))):
        target[0:ahead, :] = jnp.zeros((ahead, LANES), F32)
        target[ahead : ahead + rows, :] = values.reshape(rows, LANES)
    periods = blocks // ROW_BLOCKS
    bin_blocks = ROW_BLOCKS // owners
    for flip in range(owners):
        source, target = (series, mine) if flip == 0 else (whole, piece)
        at = 0
        for period in range(periods + 1):
            for j in range(bin_blocks + 1):
                block = ((here ^ flip) * bin_blocks + j) & (ROW_BLOCKS - 1)
                first = (period * ROW_BLOCKS + block) * trials
                target[at : at + trials, :] = source[pl.ds(first, trials), :]
                at += trials
        if flip:
            sends[flip - 1][0:at, :] = to_i16(piece[...])
            sends[flip - 1][at : at + trials, :] = to_i16(exponent)


def cut_by_phase(own, far, blocks, trials, owners):
    out_blocks = LEAD + blocks
    periods = blocks // ROW_BLOCKS
    bin_blocks = ROW_BLOCKS // owners
    rows = (periods + 1) * (bin_blocks + 1) * trials
    vmem = pl.BlockSpec(memory_space=pltpu.VMEM)
    held = (out_blocks + ROW_BLOCKS - LEAD) * trials
    return pl.pallas_call(
        functools.partial(cut_kernel, blocks, trials, owners, len(far)),
        in_specs=[vmem] * (1 + len(far)),
        out_specs=[vmem] * owners,
        out_shape=[jax.ShapeDtypeStruct((rows, LANES), F32)]
        + [jax.ShapeDtypeStruct((rows + trials, LANES), jnp.int16)] * (owners - 1),
        scratch_shapes=[
            pltpu.VMEM((held, LANES), F32),
            pltpu.VMEM((held, LANES), F32),
            pltpu.VMEM((rows, LANES), F32),
        ],
        compiler_params=pltpu.CompilerParams(vmem_limit_bytes=VMEM_LIMIT),
        name="cut",
    )(own, *far)


def fold_kernel(periods, trials, owners, widths, width_ref, mine_ref, *refs):
    parts, (ffa_ref, box_ref) = refs[: owners - 1], refs[owners - 1 : owners + 1]
    rows_in, code, folded = refs[owners + 1 :]
    here = lax.axis_index("tm")
    bin_blocks = ROW_BLOCKS // owners
    row_len = (bin_blocks + 1) * trials
    held = periods * row_len
    rows_in[0:row_len, :] = jnp.zeros((row_len, LANES), F32)
    for flip in range(owners):
        if flip == 0:
            rest = mine_ref[row_len : row_len + held, :]
        else:
            part = parts[flip - 1]
            total = row_len + held
            scale = jnp.exp2(part[total : total + trials, :].astype(F32))
            values = part[0:total, :].astype(F32)
            values = values.reshape(total // trials, trials, LANES) * scale[None]
            code[flip - 1] = values.reshape(total, LANES)
            rest = code[flip - 1, row_len : row_len + held, :]
        first = (here ^ flip) * held + row_len
        rows_in[pl.ds(first, held), :] = rest
    for flip in range(owners):
        early = mine_ref[0:row_len, :] if flip == 0 else code[flip - 1, 0:row_len, :]
        first = (here ^ flip) * held
        rows_in[pl.ds(first, row_len), :] += early

    tap = lax.broadcasted_iota(jnp.int32, (2 * LANES, LANES), 0) - lax.broadcasted_iota(
        jnp.int32, (2 * LANES, LANES), 1
    )
    bands, weights = [], []
    for w in range(widths):
        width = width_ref[w]
        inside = jnp.logical_and(tap >= 0, tap < width)
        bands.append(jnp.where(inside, 1.0, 0.0).astype(jnp.bfloat16))
        weights.append(1.0 / jnp.sqrt(jnp.full((trials, LANES), width, jnp.int32).astype(F32)))
    band = jnp.concatenate(bands, axis=1)
    lane = lane_iota(trials)
    row_count = owners * periods

    def moved(row, by):
        if by == 0:
            return row
        rolled = [pltpu.roll(block, LANES - by, 1) for block in row]
        out = []
        for b in range(bin_blocks + 1):
            after = rolled[min(b + 1, bin_blocks)]
            out.append(jnp.where(lane < LANES - by, rolled[b], after))
        return out

    for group in range(row_count // GROUP):
        rows = []
        for r in range(GROUP):
            at = (1 + group * GROUP + r) * row_len
            rows.append(
                [
                    rows_in[at + b * trials : at + (b + 1) * trials, :]
                    for b in range(bin_blocks + 1)
                ]
            )
        for level in range(LEVELS):
            half = 2**level
            new = []
            for start in range(0, GROUP, 2 * half):
                for j in range(2 * half):
                    upper = rows[start + j // 2]
                    lower = moved(rows[start + half + j // 2], (j + 1) // 2)
                    new.append([u + low for u, low in zip(upper, lower)])
            rows = new
        for r in range(GROUP):
            row = group * GROUP + r
            for b in range(bin_blocks + 1):
                at = (b * GROUP + r) * trials
                folded[at : at + trials, :] = rows[r][b]
                if b < bin_blocks:
                    first = (row // 8 * bin_blocks + b) * 8 + row % 8
                    step = row_count * bin_blocks
                    ffa_ref[pl.ds(first, trials, stride=step), :] = rows[r][b]
        span = GROUP * trials
        for b in range(bin_blocks):
            left = jnp.concatenate(
                [folded[i * span : (i + 1) * span, :] for i in (b, b + 1)], axis=1
            )
            product = None
            for _ in range(3):
                high = left.astype(jnp.bfloat16)
                left = left - high.astype(F32)
                term = jnp.dot(high, band, preferred_element_type=F32)
                product = term if product is None else product + term
            for r in range(GROUP):
                row = group * GROUP + r
                for w in range(widths):
                    value = product[
                        r * trials : (r + 1) * trials, w * LANES : (w + 1) * LANES
                    ]
                    first = (row * bin_blocks + b) * widths + w
                    step = row_count * bin_blocks * widths
                    box_ref[pl.ds(first, trials, stride=step), :] = value * weights[w]


def fold_and_box(mine, parts, box_width, periods, trials, owners):
    bin_blocks = ROW_BLOCKS // owners
    widths = box_width.shape[0]
    row_count = owners * periods
    row_len = (bin_blocks + 1) * trials
    ffa_rows = trials * row_count * bin_blocks
    vmem = pl.BlockSpec(memory_space=pltpu.VMEM)
    ffa, box = pl.pallas_call(
        functools.partial(fold_kernel, periods, trials, owners, widths),
        in_specs=[pl.BlockSpec(memory_space=pltpu.SMEM)] + [vmem] * owners,
        out_specs=[vmem, vmem],
        out_shape=[
            jax.ShapeDtypeStruct((ffa_rows, LANES), F32),
            jax.ShapeDtypeStruct((ffa_rows * widths, LANES), F32),
        ],
        scratch_shapes=[
            pltpu.VMEM(((row_count + 1) * row_len, LANES), F32),
            pltpu.VMEM((max(owners - 1, 1), (periods + 1) * row_len, LANES), F32),
            pltpu.VMEM((GROUP * row_len, LANES), F32),
        ],
        compiler_params=pltpu.CompilerParams(vmem_limit_bytes=VMEM_LIMIT),
        name="fold",
    )(box_width, mine, *parts)
    bins = bin_blocks * LANES
    ffa = ffa.reshape(trials, row_count // 8, bin_blocks, 8, LANES)
    ffa = ffa.transpose(0, 1, 3, 2, 4).reshape(trials, row_count, bins)
    box = box.reshape(trials, row_count, bin_blocks, widths, LANES)
    box = box.transpose(0, 1, 3, 2, 4).reshape(trials, row_count, widths, bins)
    return ffa, box


def per_device(filterbank, chan_delay, sub_delay, box_width):
    chan_size, owners = lax.axis_size("chan"), lax.axis_size("tm")
    samples = filterbank.shape[1]
    subs, trials = NSUB // chan_size, NDM // chan_size
    blocks, periods = samples // LANES, samples // NBIN
    quad = math.gcd(chan_size, 4)
    own = subband_sums(filterbank, chan_delay, subs)
    part = {0: own}
    for flip in range(1, quad):
        part[flip] = lax.ppermute(own, "chan", pairs(chan_size, flip))
    sizes = (blocks, subs, trials)
    flips = tuple(range(quad, chan_size, quad))
    early, final = ((0, 2), (1, 3)) if quad == 4 else ((0,), tuple(range(1, quad)))
    far, near = None, None
    for origin in early:
        both = origin == 0
        sums = trial_sums(
            [part[origin]], (origin,), sub_delay, sizes, (*flips, 0) if both else flips, far
        )
        far, near = (sums[:-1], sums[-1:]) if both else (sums, near)
    last = [part[origin] for origin in final]
    far = trial_sums(last, final, sub_delay, sizes, flips, far, True)
    far = [
        lax.ppermute(send, "chan", pairs(chan_size, flip))
        for send, flip in zip(far, flips)
    ]
    rest = (*early[1:], *final)
    (near,) = trial_sums([part[o] for o in rest], rest, sub_delay, sizes, (0,), near)
    mine, *sends = cut_by_phase(near, far, blocks, trials, owners)
    got = [
        lax.ppermute(send, "tm", pairs(owners, flip + 1))
        for flip, send in enumerate(sends)
    ]
    return fold_and_box(mine, got, box_width, periods, trials, owners)


def solution(mesh):
    placed = (P("chan", "tm"), P("chan"), P(), P())
    return jax.shard_map(
        per_device,
        mesh=mesh,
        in_specs=placed,
        out_specs=(P("chan", None, "tm"), P("chan", None, None, "tm")),
        check_vma=False,
    )
```

```python
import functools
import math

import jax
import jax.numpy as jnp
from jax import lax
from jax.experimental import pallas as pl
from jax.experimental.pallas import tpu as pltpu
from jax.sharding import PartitionSpec as P

NCHAN = 4096
NSUB = 64
NDM = 64
NBIN = 2048
LEVELS = 4
MAXW = 32
D1MAX = 128
D2MAX = 896

LANES = 128
F32 = jnp.float32
GROUP = 2**LEVELS
ROW_BLOCKS = NBIN // LANES
LEAD = (D1MAX + D2MAX) // LANES
BOX_ROWS = 4
VMEM_LIMIT = 48 << 20
SCALE = 2.0 ** (-LEVELS / 2) / math.sqrt(NCHAN)


def lane_iota(rows):
    return lax.broadcasted_iota(jnp.int32, (rows, LANES), 1)


def column_exponent(peak):
    return jnp.floor(jnp.log2(jnp.maximum(peak, 2.0**-110))) - 14.0


def scaled(values, exponent):
    return jnp.clip(jnp.round(values * jnp.exp2(-exponent)), -32767.0, 32767.0)


def to_i16(values):
    return values.astype(jnp.int32).astype(jnp.int16)


def pairs(size, flip):
    return [(i, i ^ flip) for i in range(size)]


def subband_kernel(chans, blocks, subs, delay_hbm, x_hbm, out_ref, *scratch):
    delay_ref, x_ref, turned, late, sums, x_sem, delay_sem = scratch
    delay_copy = pltpu.make_async_copy(delay_hbm, delay_ref, delay_sem)
    delay_copy.start()

    def x_copy(sub):
        return pltpu.make_async_copy(
            x_hbm.at[pl.ds(sub * chans, chans), :], x_ref.at[sub], x_sem.at[sub]
        )

    for sub in range(subs):
        x_copy(sub).start()
    delay_copy.wait()
    lane = lane_iota(8)
    tiles = blocks // 8
    pitch = blocks + 4

    @pl.loop(0, subs)
    def _(sub):
        x_copy(sub).wait()
        here = [jnp.zeros((8, LANES), F32)] * tiles
        before = [jnp.zeros((8, LANES), F32)] * tiles
        for octet in range(chans // 8):
            if octet % 2 == 0:
                for block in range(blocks):
                    both = x_ref[
                        sub,
                        8 * octet : 8 * octet + 16,
                        block * LANES : (block + 1) * LANES,
                    ].astype(F32)
                    for k in range(2):
                        base = (octet + k) * pitch * 8
                        if (octet + k) % 4 == 0:
                            at = pl.ds(base + block * 8, 8)
                        else:
                            at = pl.ds(base + block, 8, stride=pitch)
                        turned[at, :] = both[8 * k : 8 * k + 8]
            for i in range(8):
                delay = delay_ref[sub * chans + octet * 8 + i]
                shift = (2 * LANES - delay) & (LANES - 1)
                stays = lane < LANES - delay
                values = []
                for t in range(tiles):
                    base = octet * pitch * 8
                    if octet % 4 == 0:
                        at = pl.ds(base + t * 64 + i, 8, stride=8)
                    else:
                        at = pl.ds(base + i * pitch + t * 8, 8)
                    values.append(turned[at, :])
                for t in range(0, tiles, 2):
                    both = jnp.concatenate(values[t : t + 2], axis=0)
                    both = pltpu.roll(both.astype(x_ref.dtype), shift, 1).astype(F32)
                    for k in range(2):
                        value = both[8 * k : 8 * k + 8]
                        here[t + k] = here[t + k] + jnp.where(stays, value, 0.0)
                        before[t + k] = before[t + k] + jnp.where(stays, 0.0, value)
        for t in range(tiles):
            late[8 * t : 8 * t + 8, :] = before[t]
        late[blocks : blocks + 8, :] = jnp.zeros((8, LANES), F32)
        sums[pl.ds(sub, 1), :] = late[0:1, :]
        for t in range(tiles):
            sums[pl.ds((8 * t + 1) * subs + sub, 8, stride=subs), :] = (
                here[t] + late[8 * t + 1 : 8 * t + 9, :]
            )

    rows = (blocks + 1) * subs
    values = sums[...].reshape(blocks + 1, subs, LANES)
    exponent = column_exponent(jnp.max(jnp.abs(values), axis=0))
    out_ref[0:rows, :] = to_i16(scaled(values, exponent[None]).reshape(rows, LANES))
    out_ref[rows : rows + subs, :] = to_i16(exponent)


def subband_sums(filterbank, chan_delay, subs):
    chans_here, samples = filterbank.shape
    chans, blocks = chans_here // subs, samples // LANES
    rows = (blocks + 2) * subs
    return pl.pallas_call(
        functools.partial(subband_kernel, chans, blocks, subs),
        in_specs=[pl.BlockSpec(memory_space=pltpu.HBM)] * 2,
        out_specs=pl.BlockSpec(memory_space=pltpu.VMEM),
        out_shape=jax.ShapeDtypeStruct((rows, LANES), jnp.int16),
        scratch_shapes=[
            pltpu.SMEM((chans_here,), jnp.int32),
            pltpu.VMEM((subs, chans, samples), filterbank.dtype),
            pltpu.VMEM((chans * (blocks + 4), LANES), F32),
            pltpu.VMEM((blocks + 8, LANES), F32),
            pltpu.VMEM(((blocks + 1) * subs, LANES), F32),
            pltpu.SemaphoreType.DMA((subs,)),
            pltpu.SemaphoreType.DMA(()),
        ],
        compiler_params=pltpu.CompilerParams(vmem_limit_bytes=VMEM_LIMIT),
        name="subbands",
    )(pltpu.with_memory_space_constraint(chan_delay, pltpu.HBM), filterbank)


def box_taps(width_ref, band_ref, weight_ref):
    ahead = lax.broadcasted_iota(
        jnp.int32, (2 * LANES, LANES), 0
    ) - lax.broadcasted_iota(jnp.int32, (2 * LANES, LANES), 1)
    for w in range(width_ref.shape[0]):
        width = width_ref[w]
        inside = jnp.logical_and(ahead >= 0, ahead < width)
        inside = jnp.where(inside, 1.0, 0.0).astype(band_ref.dtype)
        band_ref[:, w * LANES : (w + 1) * LANES] = inside
        count = jnp.full((8, LANES), width, jnp.int32).astype(F32)
        weight_ref[8 * w : 8 * w + 8, :] = 1.0 / jnp.sqrt(count)


def trial_kernel(
    blocks, subs, trials, origins, flips, primed, coded, taps, delays, *refs
):
    refs = list(refs)
    take = lambda n: [refs.pop(0) for _ in range(n)]
    parts = take(len(origins))
    priors = take(len(flips)) if primed else []
    width_ref = take(1)[0] if taps else None
    outs = take(len(flips))
    if taps:
        box_taps(width_ref, *take(2))
    spread, late, acc, delay_ref, delay_sem = refs
    chan = lax.axis_index("chan")
    fetched = delay_ref.shape[1]
    copies, offset = [], []
    for i, flip in enumerate(flips):
        wanted = (chan ^ flip) * trials
        first = wanted // fetched * fetched
        offset.append(wanted - first)
        copies.append(
            pltpu.make_async_copy(
                delays.at[pl.ds(pl.multiple_of(first, 8), fetched), :],
                delay_ref.at[i],
                delay_sem.at[i],
            )
        )
        copies[i].start()
    out_blocks = LEAD + blocks
    depth = out_blocks + LEAD
    for at, part in enumerate(parts):
        base = at * depth * subs
        rows = (blocks + 1) * subs
        scale = jnp.exp2(part[rows : rows + subs, :].astype(F32))
        lead = (LEAD - 1) * subs
        spread[base : base + lead, :] = jnp.zeros((lead, LANES), F32)
        tail = base + lead + rows
        spread[tail : base + depth * subs, :] = jnp.zeros(
            (depth * subs - lead - rows, LANES), F32
        )
        values = part[0:rows, :].astype(F32).reshape(blocks + 1, subs, LANES)
        spread[base + lead : tail, :] = (values * scale[None]).reshape(rows, LANES)

    lane = lane_iota(8)
    tiles = out_blocks // 8

    for copy in copies:
        copy.wait()

    def one_trial(trial, i, prior, out):
        here = [jnp.zeros((8, LANES), F32)] * tiles
        before = [jnp.zeros((8, LANES), F32)] * tiles
        for at, origin in enumerate(origins):
            for sub in range(subs):
                delay = delay_ref[i, offset[i] + trial, (chan ^ origin) * subs + sub]
                shift = delay & (LANES - 1)
                stays = lane < LANES - shift
                back = (LANES - shift) & (LANES - 1)
                for t in range(tiles):
                    first = (at * depth + (delay >> 7) + 8 * t) * subs + sub
                    value = spread[pl.ds(first, 8, stride=subs), :]
                    value = pltpu.roll(value, back, 1)
                    here[t] = here[t] + jnp.where(stays, value, 0.0)
                    before[t] = before[t] + jnp.where(stays, 0.0, value)
        for t in range(tiles):
            late[8 * t : 8 * t + 8, :] = before[t]
        late[out_blocks : out_blocks + 8, :] = jnp.zeros((8, LANES), F32)
        for t in range(tiles):
            rows = pl.ds(8 * t * trials + trial, 8, stride=trials)
            value = here[t] + late[8 * t + 1 : 8 * t + 9, :]
            out[rows, :] = value if prior is None else value + prior[rows, :]

    rows = out_blocks * trials
    for i, (flip, out) in enumerate(zip(flips, outs)):
        target = acc if coded else out

        @pl.loop(0, trials, unroll=trials)
        def _(trial):
            one_trial(trial, i, priors[i] if primed else None, target)

        if coded:
            values = acc[...].reshape(out_blocks, trials, LANES)
            exponent = column_exponent(jnp.max(jnp.abs(values), axis=0))
            out[0:rows, :] = to_i16(
                scaled(values, exponent[None]).reshape(rows, LANES)
            )
            out[rows : rows + trials, :] = to_i16(exponent)


def trial_sums(
    parts, origins, sub_delay, sizes, flips, priors=None, coded=False, box_width=None
):
    if not flips:
        return []
    blocks, subs, trials = sizes
    out_blocks = LEAD + blocks
    depth = out_blocks + LEAD
    rows = out_blocks * trials
    out = jax.ShapeDtypeStruct(
        (rows + trials if coded else rows, LANES), jnp.int16 if coded else F32
    )
    vmem = pl.BlockSpec(memory_space=pltpu.VMEM)
    arrays = [*parts, *(priors or [])]
    in_specs = [pl.BlockSpec(memory_space=pl.ANY)] + [vmem] * len(arrays)
    outs = [out] * len(flips)
    taps = box_width is not None
    if taps:
        widths = box_width.shape[0]
        arrays.append(box_width)
        in_specs.append(pl.BlockSpec(memory_space=pltpu.SMEM))
        outs.append(jax.ShapeDtypeStruct((2 * LANES, widths * LANES), jnp.bfloat16))
        outs.append(jax.ShapeDtypeStruct((widths * 8, LANES), F32))
    return pl.pallas_call(
        functools.partial(
            trial_kernel, *sizes, tuple(origins), tuple(flips), bool(priors), coded, taps
        ),
        in_specs=in_specs,
        out_specs=[vmem] * len(outs),
        out_shape=outs,
        scratch_shapes=[
            pltpu.VMEM((len(parts) * depth * subs, LANES), F32),
            pltpu.VMEM((out_blocks + 8, LANES), F32),
            pltpu.VMEM((rows, LANES), F32),
            pltpu.SMEM((len(flips), max(trials, 8), sub_delay.shape[1]), jnp.int32),
            pltpu.SemaphoreType.DMA((len(flips),)),
        ],
        compiler_params=pltpu.CompilerParams(vmem_limit_bytes=VMEM_LIMIT),
        name="trials_coded" if coded else "trials",
    )(sub_delay, *arrays)


def cut_kernel(blocks, trials, owners, n_far, own_ref, *refs):
    far, mine, sends = refs[:n_far], refs[n_far], refs[n_far + 1 : n_far + owners]
    series, whole, piece = refs[n_far + owners :]
    here = lax.axis_index("tm")
    out_blocks = LEAD + blocks
    rows = out_blocks * trials
    total = own_ref[...].reshape(out_blocks, trials, LANES)
    for part in far:
        scale = jnp.exp2(part[rows : rows + trials, :].astype(F32))
        values = part[0:rows, :].astype(F32).reshape(out_blocks, trials, LANES)
        total = total + values * scale[None]
    total = total * SCALE
    ahead = (ROW_BLOCKS - LEAD) * trials
    exponent = column_exponent(jnp.max(jnp.abs(total), axis=0))
    for target, values in ((series, total), (whole, scaled(total, exponent[None]))):
        target[0:ahead, :] = jnp.zeros((ahead, LANES), F32)
        target[ahead : ahead + rows, :] = values.reshape(rows, LANES)
    periods = blocks // ROW_BLOCKS
    bin_blocks = ROW_BLOCKS // owners
    for flip in range(owners):
        source, target = (series, mine) if flip == 0 else (whole, piece)
        at = 0
        for period in range(periods + 1):
            for j in range(bin_blocks + 1):
                block = ((here ^ flip) * bin_blocks + j) & (ROW_BLOCKS - 1)
                first = (period * ROW_BLOCKS + block) * trials
                target[at : at + trials, :] = source[pl.ds(first, trials), :]
                at += trials
        if flip:
            sends[flip - 1][0:at, :] = to_i16(piece[...])
            sends[flip - 1][at : at + trials, :] = to_i16(exponent)


def cut_by_phase(own, far, blocks, trials, owners):
    out_blocks = LEAD + blocks
    periods = blocks // ROW_BLOCKS
    bin_blocks = ROW_BLOCKS // owners
    rows = (periods + 1) * (bin_blocks + 1) * trials
    vmem = pl.BlockSpec(memory_space=pltpu.VMEM)
    held = (out_blocks + ROW_BLOCKS - LEAD) * trials
    return pl.pallas_call(
        functools.partial(cut_kernel, blocks, trials, owners, len(far)),
        in_specs=[vmem] * (1 + len(far)),
        out_specs=[vmem] * owners,
        out_shape=[jax.ShapeDtypeStruct((rows, LANES), F32)]
        + [jax.ShapeDtypeStruct((rows + trials, LANES), jnp.int16)] * (owners - 1),
        scratch_shapes=[
            pltpu.VMEM((held, LANES), F32),
            pltpu.VMEM((held, LANES), F32),
            pltpu.VMEM((rows, LANES), F32),
        ],
        compiler_params=pltpu.CompilerParams(vmem_limit_bytes=VMEM_LIMIT),
        name="cut",
    )(own, *far)


def fold_kernel(periods, trials, owners, widths, band_ref, weight_ref, mine_ref, *refs):
    parts, (ffa_hbm, box_hbm) = refs[: owners - 1], refs[owners - 1 : owners + 1]
    rows_in, code, left, ffa_ref, box_ref, ffa_sem, box_sem = refs[owners + 1 :]
    here = lax.axis_index("tm")
    bin_blocks = ROW_BLOCKS // owners
    row_len = (bin_blocks + 1) * trials
    held = periods * row_len
    rows_in[0:row_len, :] = jnp.zeros((row_len, LANES), F32)
    for flip in range(owners):
        if flip == 0:
            rest = mine_ref[row_len : row_len + held, :]
        else:
            part = parts[flip - 1]
            total = row_len + held
            scale = jnp.exp2(part[total : total + trials, :].astype(F32))
            values = part[0:total, :].astype(F32)
            values = values.reshape(total // trials, trials, LANES) * scale[None]
            code[flip - 1] = values.reshape(total, LANES)
            rest = code[flip - 1, row_len : row_len + held, :]
        first = (here ^ flip) * held + row_len
        rows_in[pl.ds(first, held), :] = rest
    for flip in range(owners):
        early = mine_ref[0:row_len, :] if flip == 0 else code[flip - 1, 0:row_len, :]
        first = (here ^ flip) * held
        rows_in[pl.ds(first, row_len), :] += early

    band = band_ref[...]
    weights = [weight_ref[8 * w : 8 * w + trials, :] for w in range(widths)]
    lane = lane_iota(trials)
    row_count = owners * periods
    copies = []

    def moved(row, by):
        if by == 0:
            return row
        rolled = [pltpu.roll(block, LANES - by, 1) for block in row]
        out = []
        for b in range(bin_blocks + 1):
            after = rolled[min(b + 1, bin_blocks)]
            out.append(jnp.where(lane < LANES - by, rolled[b], after))
        return out

    def leave(held_ref, hbm, sem, per_trial, first, size):
        for k in range(trials):
            at = pl.ds(k * per_trial + first, size)
            piece = k * (per_trial // size) + first // size
            copies.append(
                pltpu.make_async_copy(held_ref.at[at, :], hbm.at[at, :], sem.at[piece])
            )
            copies[-1].start()

    for group in range(row_count // GROUP):
        rows = []
        for r in range(GROUP):
            at = (1 + group * GROUP + r) * row_len
            rows.append(
                [
                    rows_in[at + b * trials : at + (b + 1) * trials, :]
                    for b in range(bin_blocks + 1)
                ]
            )
        for level in range(LEVELS):
            half = 2**level
            new = []
            for start in range(0, GROUP, 2 * half):
                for j in range(2 * half):
                    upper = rows[start + j // 2]
                    lower = moved(rows[start + half + j // 2], (j + 1) // 2)
                    new.append([u + low for u, low in zip(upper, lower)])
            rows = new
        for r in range(GROUP):
            row = group * GROUP + r
            for b in range(bin_blocks):
                at = (r * bin_blocks + b) * trials
                left[at : at + trials, 0:LANES] = rows[r][b]
                left[at : at + trials, LANES : 2 * LANES] = rows[r][b + 1]
                first = (row // 8 * bin_blocks + b) * 8 + row % 8
                step = row_count * bin_blocks
                ffa_ref[pl.ds(first, trials, stride=step), :] = rows[r][b]
        per_trial = row_count * bin_blocks
        size = GROUP * bin_blocks
        leave(ffa_ref, ffa_hbm, ffa_sem, per_trial, group * size, size)
        for start in range(0, GROUP, BOX_ROWS):
            lines = bin_blocks * trials
            rest = left[start * lines : (start + BOX_ROWS) * lines, :]
            product = None
            for _ in range(2):
                high = rest.astype(jnp.bfloat16)
                rest = rest - high.astype(F32)
                term = jnp.dot(high, band, preferred_element_type=F32)
                product = term if product is None else product + term
            step = row_count * bin_blocks * widths
            for i in range(BOX_ROWS * bin_blocks):
                for w in range(widths):
                    value = product[
                        i * trials : (i + 1) * trials, w * LANES : (w + 1) * LANES
                    ]
                    line = (group * GROUP + start) * bin_blocks + i
                    first = line * widths + w
                    box_ref[pl.ds(first, trials, stride=step), :] = value * weights[w]
            size = BOX_ROWS * bin_blocks * widths
            leave(box_ref, box_hbm, box_sem, step, (group * GROUP + start) // BOX_ROWS * size, size)
    for copy in copies:
        copy.wait()


def fold_and_box(mine, parts, taps, periods, trials, owners):
    bin_blocks = ROW_BLOCKS // owners
    widths = taps[0].shape[1] // LANES
    row_count = owners * periods
    row_len = (bin_blocks + 1) * trials
    ffa_rows = trials * row_count * bin_blocks
    ffa_shape = jax.ShapeDtypeStruct((ffa_rows, LANES), F32)
    box_shape = jax.ShapeDtypeStruct((ffa_rows * widths, LANES), F32)
    vmem = pl.BlockSpec(memory_space=pltpu.VMEM)
    anywhere = pl.BlockSpec(memory_space=pl.ANY)
    ffa, box = pl.pallas_call(
        functools.partial(fold_kernel, periods, trials, owners, widths),
        in_specs=[vmem] * (2 + owners),
        out_specs=[anywhere, anywhere],
        out_shape=[ffa_shape, box_shape],
        scratch_shapes=[
            pltpu.VMEM(((row_count + 1) * row_len, LANES), F32),
            pltpu.VMEM((max(owners - 1, 1), (periods + 1) * row_len, LANES), F32),
            pltpu.VMEM((GROUP * bin_blocks * trials, 2 * LANES), F32),
            pltpu.VMEM(ffa_shape.shape, F32),
            pltpu.VMEM(box_shape.shape, F32),
            pltpu.SemaphoreType.DMA((trials * row_count // GROUP,)),
            pltpu.SemaphoreType.DMA((trials * row_count // BOX_ROWS,)),
        ],
        compiler_params=pltpu.CompilerParams(vmem_limit_bytes=VMEM_LIMIT),
        name="fold",
    )(*taps, mine, *parts)
    bins = bin_blocks * LANES
    ffa = ffa.reshape(trials, row_count // 8, bin_blocks, 8, LANES)
    ffa = ffa.transpose(0, 1, 3, 2, 4).reshape(trials, row_count, bins)
    box = box.reshape(trials, row_count, bin_blocks, widths, LANES)
    box = box.transpose(0, 1, 3, 2, 4).reshape(trials, row_count, widths, bins)
    return ffa, box


def per_device(filterbank, chan_delay, sub_delay, box_width):
    chan_size, owners = lax.axis_size("chan"), lax.axis_size("tm")
    samples = filterbank.shape[1]
    subs, trials = NSUB // chan_size, NDM // chan_size
    blocks, periods = samples // LANES, samples // NBIN
    quad = math.gcd(chan_size, 4)
    own = subband_sums(filterbank, chan_delay, subs)
    part = {0: own}
    for flip in range(1, quad):
        part[flip] = lax.ppermute(own, "chan", pairs(chan_size, flip))
    sizes = (blocks, subs, trials)
    flips = tuple(range(quad, chan_size, quad))
    early, final = ((0, 2, 1), (3,)) if quad == 4 else ((0,), tuple(range(1, quad)))
    far, near = None, None
    for origin in early:
        both = origin == 0
        sums = trial_sums(
            [part[origin]], (origin,), sub_delay, sizes, (*flips, 0) if both else flips, far
        )
        far, near = (sums[:-1], sums[-1:]) if both else (sums, near)
    last = [part[origin] for origin in final]
    far = trial_sums(last, final, sub_delay, sizes, flips, far, True)
    far = [
        lax.ppermute(send, "chan", pairs(chan_size, flip))
        for send, flip in zip(far, flips)
    ]
    rest = (*early[1:], *final)
    near, *taps = trial_sums(
        [part[o] for o in rest], rest, sub_delay, sizes, (0,), near, box_width=box_width
    )
    mine, *sends = cut_by_phase(near, far, blocks, trials, owners)
    got = [
        lax.ppermute(send, "tm", pairs(owners, flip + 1))
        for flip, send in enumerate(sends)
    ]
    return fold_and_box(mine, got, taps, periods, trials, owners)


def solution(mesh):
    placed = (P("chan", "tm"), P("chan"), P(), P())
    return jax.shard_map(
        per_device,
        mesh=mesh,
        in_specs=placed,
        out_specs=(P("chan", None, "tm"), P("chan", None, None, "tm")),
        check_vma=False,
    )
```

```python
import functools
import math

import jax
import jax.numpy as jnp
from jax import lax
from jax.experimental import pallas as pl
from jax.experimental.pallas import tpu as pltpu
from jax.sharding import PartitionSpec as P

NCHAN = 4096
NSUB = 64
NDM = 64
NBIN = 2048
LEVELS = 4
MAXW = 32
D1MAX = 128
D2MAX = 896

LANES = 128
F32 = jnp.float32
GROUP = 2**LEVELS
ROW_BLOCKS = NBIN // LANES
LEAD = (D1MAX + D2MAX) // LANES
BOX_ROWS = 4
VMEM_LIMIT = 48 << 20
SCALE = 2.0 ** (-LEVELS / 2) / math.sqrt(NCHAN)


def lane_iota(rows):
    return lax.broadcasted_iota(jnp.int32, (rows, LANES), 1)


def column_exponent(peak):
    return jnp.floor(jnp.log2(jnp.maximum(peak, 2.0**-110))) - 14.0


def scaled(values, exponent):
    return jnp.clip(jnp.round(values * jnp.exp2(-exponent)), -32767.0, 32767.0)


def to_i16(values):
    return values.astype(jnp.int32).astype(jnp.int16)


def pairs(size, flip):
    return [(i, i ^ flip) for i in range(size)]


def subband_kernel(chans, blocks, subs, delay_hbm, x_hbm, out_ref, *scratch):
    delay_ref, x_ref, turned, late, sums, x_sem, delay_sem = scratch
    delay_copy = pltpu.make_async_copy(delay_hbm, delay_ref, delay_sem)
    delay_copy.start()

    def x_copy(sub):
        return pltpu.make_async_copy(
            x_hbm.at[pl.ds(sub * chans, chans), :], x_ref.at[sub], x_sem.at[sub]
        )

    for sub in range(subs):
        x_copy(sub).start()
    delay_copy.wait()
    lane = lane_iota(8)
    tiles = blocks // 8
    pitch = blocks + 4

    @pl.loop(0, subs)
    def _(sub):
        x_copy(sub).wait()
        here = [jnp.zeros((8, LANES), F32)] * tiles
        before = [jnp.zeros((8, LANES), F32)] * tiles
        for octet in range(chans // 8):
            if octet % 2 == 0:
                for block in range(blocks):
                    both = x_ref[
                        sub,
                        8 * octet : 8 * octet + 16,
                        block * LANES : (block + 1) * LANES,
                    ].astype(F32)
                    for k in range(2):
                        base = (octet + k) * pitch * 8
                        if (octet + k) % 4 == 0:
                            at = pl.ds(base + block * 8, 8)
                        else:
                            at = pl.ds(base + block, 8, stride=pitch)
                        turned[at, :] = both[8 * k : 8 * k + 8]
            for i in range(8):
                delay = delay_ref[sub * chans + octet * 8 + i]
                shift = (2 * LANES - delay) & (LANES - 1)
                stays = lane < LANES - delay
                values = []
                for t in range(tiles):
                    base = octet * pitch * 8
                    if octet % 4 == 0:
                        at = pl.ds(base + t * 64 + i, 8, stride=8)
                    else:
                        at = pl.ds(base + i * pitch + t * 8, 8)
                    values.append(turned[at, :])
                for t in range(0, tiles, 2):
                    both = jnp.concatenate(values[t : t + 2], axis=0)
                    both = pltpu.roll(both.astype(x_ref.dtype), shift, 1).astype(F32)
                    for k in range(2):
                        value = both[8 * k : 8 * k + 8]
                        here[t + k] = here[t + k] + jnp.where(stays, value, 0.0)
                        before[t + k] = before[t + k] + jnp.where(stays, 0.0, value)
        for t in range(tiles):
            late[8 * t : 8 * t + 8, :] = before[t]
        late[blocks : blocks + 8, :] = jnp.zeros((8, LANES), F32)
        sums[pl.ds(sub, 1), :] = late[0:1, :]
        for t in range(tiles):
            sums[pl.ds((8 * t + 1) * subs + sub, 8, stride=subs), :] = (
                here[t] + late[8 * t + 1 : 8 * t + 9, :]
            )

    rows = (blocks + 1) * subs
    values = sums[...].reshape(blocks + 1, subs, LANES)
    exponent = column_exponent(jnp.max(jnp.abs(values), axis=0))
    out_ref[0:rows, :] = to_i16(scaled(values, exponent[None]).reshape(rows, LANES))
    out_ref[rows : rows + subs, :] = to_i16(exponent)


def subband_sums(filterbank, chan_delay, subs):
    chans_here, samples = filterbank.shape
    chans, blocks = chans_here // subs, samples // LANES
    rows = (blocks + 2) * subs
    return pl.pallas_call(
        functools.partial(subband_kernel, chans, blocks, subs),
        in_specs=[pl.BlockSpec(memory_space=pltpu.HBM)] * 2,
        out_specs=pl.BlockSpec(memory_space=pltpu.VMEM),
        out_shape=jax.ShapeDtypeStruct((rows, LANES), jnp.int16),
        scratch_shapes=[
            pltpu.SMEM((chans_here,), jnp.int32),
            pltpu.VMEM((subs, chans, samples), filterbank.dtype),
            pltpu.VMEM((chans * (blocks + 4), LANES), F32),
            pltpu.VMEM((blocks + 8, LANES), F32),
            pltpu.VMEM(((blocks + 1) * subs, LANES), F32),
            pltpu.SemaphoreType.DMA((subs,)),
            pltpu.SemaphoreType.DMA(()),
        ],
        compiler_params=pltpu.CompilerParams(vmem_limit_bytes=VMEM_LIMIT),
        name="subbands",
    )(pltpu.with_memory_space_constraint(chan_delay, pltpu.HBM), filterbank)


def box_taps(width_ref, band_ref, weight_ref):
    ahead = lax.broadcasted_iota(
        jnp.int32, (2 * LANES, LANES), 0
    ) - lax.broadcasted_iota(jnp.int32, (2 * LANES, LANES), 1)
    for w in range(width_ref.shape[0]):
        width = width_ref[w]
        inside = jnp.logical_and(ahead >= 0, ahead < width)
        inside = jnp.where(inside, 1.0, 0.0).astype(band_ref.dtype)
        band_ref[:, w * LANES : (w + 1) * LANES] = inside
        count = jnp.full((8, LANES), width, jnp.int32).astype(F32)
        weight_ref[8 * w : 8 * w + 8, :] = 1.0 / jnp.sqrt(count)


def trial_kernel(blocks, subs, trials, sides, primed, coded, taps, delays, *refs):
    refs = list(refs)
    take = lambda n: [refs.pop(0) for _ in range(n)]
    n_in, n_out = (len(each) for each in sides[0])
    parts = take(n_in)
    priors = take(n_out) if primed else [None] * n_out
    width_ref = take(1)[0] if taps else None
    outs = take(n_out)
    if taps:
        box_taps(width_ref, *take(2))
    spread, late, acc, delay_ref, delay_sem = refs
    chan = lax.axis_index("chan")
    out_blocks = LEAD + blocks
    depth = out_blocks + LEAD
    fetched = delay_ref.shape[1]
    lane = lane_iota(8)
    tiles = out_blocks // 8

    def on_side(origins, flips):
        copies, offset = {}, {}
        for i, flip in enumerate(flips):
            if flip is None:
                continue
            wanted = (chan ^ flip) * trials
            first = wanted // fetched * fetched
            offset[i] = wanted - first
            copies[i] = pltpu.make_async_copy(
                delays.at[pl.ds(pl.multiple_of(first, 8), fetched), :],
                delay_ref.at[i],
                delay_sem.at[i],
            )
            copies[i].start()
        for at, (origin, part) in enumerate(zip(origins, parts)):
            if origin is None:
                continue
            base = at * depth * subs
            rows = (blocks + 1) * subs
            scale = jnp.exp2(part[rows : rows + subs, :].astype(F32))
            lead = (LEAD - 1) * subs
            spread[base : base + lead, :] = jnp.zeros((lead, LANES), F32)
            tail = base + lead + rows
            spread[tail : base + depth * subs, :] = jnp.zeros(
                (depth * subs - lead - rows, LANES), F32
            )
            values = part[0:rows, :].astype(F32).reshape(blocks + 1, subs, LANES)
            spread[base + lead : tail, :] = (values * scale[None]).reshape(rows, LANES)
        for copy in copies.values():
            copy.wait()

        def one_trial(trial, i, prior, out):
            here = [jnp.zeros((8, LANES), F32)] * tiles
            before = [jnp.zeros((8, LANES), F32)] * tiles
            for at, origin in enumerate(origins):
                if origin is None:
                    continue
                for sub in range(subs):
                    column = (chan ^ origin) * subs + sub
                    delay = delay_ref[i, offset[i] + trial, column]
                    shift = delay & (LANES - 1)
                    stays = lane < LANES - shift
                    back = (LANES - shift) & (LANES - 1)
                    for t in range(tiles):
                        first = (at * depth + (delay >> 7) + 8 * t) * subs + sub
                        value = spread[pl.ds(first, 8, stride=subs), :]
                        value = pltpu.roll(value, back, 1)
                        here[t] = here[t] + jnp.where(stays, value, 0.0)
                        before[t] = before[t] + jnp.where(stays, 0.0, value)
            for t in range(tiles):
                late[8 * t : 8 * t + 8, :] = before[t]
            late[out_blocks : out_blocks + 8, :] = jnp.zeros((8, LANES), F32)
            for t in range(tiles):
                rows = pl.ds(8 * t * trials + trial, 8, stride=trials)
                value = here[t] + late[8 * t + 1 : 8 * t + 9, :]
                out[rows, :] = value if prior is None else value + prior[rows, :]

        rows = out_blocks * trials
        nothing_new = all(origin is None for origin in origins)
        for i, (flip, prior, out) in enumerate(zip(flips, priors, outs)):
            if flip is None:
                continue
            result = acc if coded else out
            if nothing_new:
                result = prior
            else:

                @pl.loop(0, trials, unroll=trials)
                def _(trial):
                    one_trial(trial, i, prior, result)

            if coded:
                values = result[...].reshape(out_blocks, trials, LANES)
                exponent = column_exponent(jnp.max(jnp.abs(values), axis=0))
                out[0:rows, :] = to_i16(
                    scaled(values, exponent[None]).reshape(rows, LANES)
                )
                out[rows : rows + trials, :] = to_i16(exponent)
            elif nothing_new:
                out[...] = prior[...]

    if sides[0] == sides[1]:
        on_side(*sides[0])
    else:
        core = lax.axis_index("tm") & 1
        for each, side in enumerate(sides):

            @pl.when(core == each)
            def _():
                on_side(*side)


def trial_sums(
    parts, origins, sub_delay, sizes, flips, priors=None, coded=False, box_width=None
):
    blocks, subs, trials = sizes
    n_out = len(flips[0])
    out_blocks = LEAD + blocks
    depth = out_blocks + LEAD
    rows = out_blocks * trials
    out = jax.ShapeDtypeStruct(
        (rows + trials if coded else rows, LANES), jnp.int16 if coded else F32
    )
    vmem = pl.BlockSpec(memory_space=pltpu.VMEM)
    arrays = [*parts, *(priors or [])]
    in_specs = [pl.BlockSpec(memory_space=pl.ANY)] + [vmem] * len(arrays)
    outs = [out] * n_out
    taps = box_width is not None
    if taps:
        widths = box_width.shape[0]
        arrays.append(box_width)
        in_specs.append(pl.BlockSpec(memory_space=pltpu.SMEM))
        outs.append(jax.ShapeDtypeStruct((2 * LANES, widths * LANES), jnp.bfloat16))
        outs.append(jax.ShapeDtypeStruct((widths * 8, LANES), F32))
    return pl.pallas_call(
        functools.partial(
            trial_kernel, *sizes, tuple(zip(origins, flips)), bool(priors), coded, taps
        ),
        in_specs=in_specs,
        out_specs=[vmem] * len(outs),
        out_shape=outs,
        scratch_shapes=[
            pltpu.VMEM((len(parts) * depth * subs, LANES), F32),
            pltpu.VMEM((out_blocks + 8, LANES), F32),
            pltpu.VMEM((rows, LANES), F32),
            pltpu.SMEM((n_out, max(trials, 8), sub_delay.shape[1]), jnp.int32),
            pltpu.SemaphoreType.DMA((n_out,)),
        ],
        compiler_params=pltpu.CompilerParams(vmem_limit_bytes=VMEM_LIMIT),
        name="trials_coded" if coded else "trials",
    )(sub_delay, *arrays)


def cut_kernel(blocks, trials, owners, n_far, own_ref, *refs):
    far, mine, sends = refs[:n_far], refs[n_far], refs[n_far + 1 : n_far + owners]
    series, whole, piece = refs[n_far + owners :]
    here = lax.axis_index("tm")
    out_blocks = LEAD + blocks
    rows = out_blocks * trials
    total = own_ref[...].reshape(out_blocks, trials, LANES)
    for part in far:
        scale = jnp.exp2(part[rows : rows + trials, :].astype(F32))
        values = part[0:rows, :].astype(F32).reshape(out_blocks, trials, LANES)
        total = total + values * scale[None]
    total = total * SCALE
    ahead = (ROW_BLOCKS - LEAD) * trials
    exponent = column_exponent(jnp.max(jnp.abs(total), axis=0))
    for target, values in ((series, total), (whole, scaled(total, exponent[None]))):
        target[0:ahead, :] = jnp.zeros((ahead, LANES), F32)
        target[ahead : ahead + rows, :] = values.reshape(rows, LANES)
    periods = blocks // ROW_BLOCKS
    bin_blocks = ROW_BLOCKS // owners
    for flip in range(owners):
        source, target = (series, mine) if flip == 0 else (whole, piece)
        at = 0
        for period in range(periods + 1):
            for j in range(bin_blocks + 1):
                block = ((here ^ flip) * bin_blocks + j) & (ROW_BLOCKS - 1)
                first = (period * ROW_BLOCKS + block) * trials
                target[at : at + trials, :] = source[pl.ds(first, trials), :]
                at += trials
        if flip:
            sends[flip - 1][0:at, :] = to_i16(piece[...])
            sends[flip - 1][at : at + trials, :] = to_i16(exponent)


def cut_by_phase(own, far, blocks, trials, owners):
    out_blocks = LEAD + blocks
    periods = blocks // ROW_BLOCKS
    bin_blocks = ROW_BLOCKS // owners
    rows = (periods + 1) * (bin_blocks + 1) * trials
    vmem = pl.BlockSpec(memory_space=pltpu.VMEM)
    held = (out_blocks + ROW_BLOCKS - LEAD) * trials
    return pl.pallas_call(
        functools.partial(cut_kernel, blocks, trials, owners, len(far)),
        in_specs=[vmem] * (1 + len(far)),
        out_specs=[vmem] * owners,
        out_shape=[jax.ShapeDtypeStruct((rows, LANES), F32)]
        + [jax.ShapeDtypeStruct((rows + trials, LANES), jnp.int16)] * (owners - 1),
        scratch_shapes=[
            pltpu.VMEM((held, LANES), F32),
            pltpu.VMEM((held, LANES), F32),
            pltpu.VMEM((rows, LANES), F32),
        ],
        compiler_params=pltpu.CompilerParams(vmem_limit_bytes=VMEM_LIMIT),
        name="cut",
    )(own, *far)


def fold_kernel(periods, trials, owners, widths, band_ref, weight_ref, mine_ref, *refs):
    parts, (ffa_hbm, box_hbm) = refs[: owners - 1], refs[owners - 1 : owners + 1]
    rows_in, code, left, ffa_ref, box_ref, ffa_sem, box_sem = refs[owners + 1 :]
    here = lax.axis_index("tm")
    bin_blocks = ROW_BLOCKS // owners
    row_len = (bin_blocks + 1) * trials
    held = periods * row_len
    rows_in[0:row_len, :] = jnp.zeros((row_len, LANES), F32)
    for flip in range(owners):
        if flip == 0:
            rest = mine_ref[row_len : row_len + held, :]
        else:
            part = parts[flip - 1]
            total = row_len + held
            scale = jnp.exp2(part[total : total + trials, :].astype(F32))
            values = part[0:total, :].astype(F32)
            values = values.reshape(total // trials, trials, LANES) * scale[None]
            code[flip - 1] = values.reshape(total, LANES)
            rest = code[flip - 1, row_len : row_len + held, :]
        first = (here ^ flip) * held + row_len
        rows_in[pl.ds(first, held), :] = rest
    for flip in range(owners):
        early = mine_ref[0:row_len, :] if flip == 0 else code[flip - 1, 0:row_len, :]
        first = (here ^ flip) * held
        rows_in[pl.ds(first, row_len), :] += early

    band = band_ref[...]
    weights = [weight_ref[8 * w : 8 * w + trials, :] for w in range(widths)]
    lane = lane_iota(trials)
    row_count = owners * periods
    copies = []

    def moved(row, by):
        if by == 0:
            return row
        rolled = [pltpu.roll(block, LANES - by, 1) for block in row]
        out = []
        for b in range(bin_blocks + 1):
            after = rolled[min(b + 1, bin_blocks)]
            out.append(jnp.where(lane < LANES - by, rolled[b], after))
        return out

    def leave(held_ref, hbm, sem, per_trial, first, size):
        for k in range(trials):
            at = pl.ds(k * per_trial + first, size)
            piece = k * (per_trial // size) + first // size
            copies.append(
                pltpu.make_async_copy(held_ref.at[at, :], hbm.at[at, :], sem.at[piece])
            )
            copies[-1].start()

    for group in range(row_count // GROUP):
        rows = []
        for r in range(GROUP):
            at = (1 + group * GROUP + r) * row_len
            rows.append(
                [
                    rows_in[at + b * trials : at + (b + 1) * trials, :]
                    for b in range(bin_blocks + 1)
                ]
            )
        for level in range(LEVELS):
            half = 2**level
            new = []
            for start in range(0, GROUP, 2 * half):
                for j in range(2 * half):
                    upper = rows[start + j // 2]
                    lower = moved(rows[start + half + j // 2], (j + 1) // 2)
                    new.append([u + low for u, low in zip(upper, lower)])
            rows = new
        for r in range(GROUP):
            row = group * GROUP + r
            for b in range(bin_blocks):
                at = (r * bin_blocks + b) * trials
                left[at : at + trials, 0:LANES] = rows[r][b]
                left[at : at + trials, LANES : 2 * LANES] = rows[r][b + 1]
                first = (row // 8 * bin_blocks + b) * 8 + row % 8
                step = row_count * bin_blocks
                ffa_ref[pl.ds(first, trials, stride=step), :] = rows[r][b]
        per_trial = row_count * bin_blocks
        size = GROUP * bin_blocks
        leave(ffa_ref, ffa_hbm, ffa_sem, per_trial, group * size, size)
        for start in range(0, GROUP, BOX_ROWS):
            lines = bin_blocks * trials
            rest = left[start * lines : (start + BOX_ROWS) * lines, :]
            product = None
            for _ in range(2):
                high = rest.astype(jnp.bfloat16)
                rest = rest - high.astype(F32)
                term = jnp.dot(high, band, preferred_element_type=F32)
                product = term if product is None else product + term
            step = row_count * bin_blocks * widths
            for i in range(BOX_ROWS * bin_blocks):
                for w in range(widths):
                    value = product[
                        i * trials : (i + 1) * trials, w * LANES : (w + 1) * LANES
                    ]
                    line = (group * GROUP + start) * bin_blocks + i
                    first = line * widths + w
                    box_ref[pl.ds(first, trials, stride=step), :] = value * weights[w]
            size = BOX_ROWS * bin_blocks * widths
            leave(box_ref, box_hbm, box_sem, step, (group * GROUP + start) // BOX_ROWS * size, size)
    for copy in copies:
        copy.wait()


def fold_and_box(mine, parts, taps, periods, trials, owners):
    bin_blocks = ROW_BLOCKS // owners
    widths = taps[0].shape[1] // LANES
    row_count = owners * periods
    row_len = (bin_blocks + 1) * trials
    ffa_rows = trials * row_count * bin_blocks
    ffa_shape = jax.ShapeDtypeStruct((ffa_rows, LANES), F32)
    box_shape = jax.ShapeDtypeStruct((ffa_rows * widths, LANES), F32)
    vmem = pl.BlockSpec(memory_space=pltpu.VMEM)
    anywhere = pl.BlockSpec(memory_space=pl.ANY)
    ffa, box = pl.pallas_call(
        functools.partial(fold_kernel, periods, trials, owners, widths),
        in_specs=[vmem] * (2 + owners),
        out_specs=[anywhere, anywhere],
        out_shape=[ffa_shape, box_shape],
        scratch_shapes=[
            pltpu.VMEM(((row_count + 1) * row_len, LANES), F32),
            pltpu.VMEM((max(owners - 1, 1), (periods + 1) * row_len, LANES), F32),
            pltpu.VMEM((GROUP * bin_blocks * trials, 2 * LANES), F32),
            pltpu.VMEM(ffa_shape.shape, F32),
            pltpu.VMEM(box_shape.shape, F32),
            pltpu.SemaphoreType.DMA((trials * row_count // GROUP,)),
            pltpu.SemaphoreType.DMA((trials * row_count // BOX_ROWS,)),
        ],
        compiler_params=pltpu.CompilerParams(vmem_limit_bytes=VMEM_LIMIT),
        name="fold",
    )(*taps, mine, *parts)
    bins = bin_blocks * LANES
    ffa = ffa.reshape(trials, row_count // 8, bin_blocks, 8, LANES)
    ffa = ffa.transpose(0, 1, 3, 2, 4).reshape(trials, row_count, bins)
    box = box.reshape(trials, row_count, bin_blocks, widths, LANES)
    box = box.transpose(0, 1, 3, 2, 4).reshape(trials, row_count, widths, bins)
    return ffa, box


def per_device(filterbank, chan_delay, sub_delay, box_width):
    chan_size, owners = lax.axis_size("chan"), lax.axis_size("tm")
    samples = filterbank.shape[1]
    subs, trials = NSUB // chan_size, NDM // chan_size
    blocks, periods = samples // LANES, samples // NBIN
    own = subband_sums(filterbank, chan_delay, subs)

    quad = math.gcd(chan_size, 4)
    near_by, across = list(range(1, quad)), list(range(quad, chan_size, quad))
    slots = max(len(near_by), len(across))
    near_by += [None] * (slots - len(near_by))
    across += [None] * (slots - len(across))
    origins, targets = (across, near_by), (near_by, across)

    def swapped(array, flips):
        route = []
        for tm in range(owners):
            if flips[tm & 1] is not None:
                for chan in range(chan_size):
                    route.append(
                        (chan * owners + tm, (chan ^ flips[tm & 1]) * owners + tm)
                    )
        return lax.ppermute(array, ("chan", "tm"), route)

    got = [
        swapped(own, (origins[0][slot], origins[1][slot])) for slot in range(slots)
    ]
    sizes = (blocks, subs, trials)
    sends = tuple(map(tuple, targets))
    both = lambda *values: (values, values)
    first = lambda at, until: tuple(tuple(each[at:until]) for each in origins)
    *sums, near = trial_sums(
        [own], both(0), sub_delay, sizes, tuple((*each, 0) for each in sends)
    )
    if slots > 1:
        sums = trial_sums(got[:1], first(0, 1), sub_delay, sizes, sends, sums)
    rest = min(slots - 1, 1)
    sums = trial_sums(
        got[rest:], first(rest, slots), sub_delay, sizes, sends, sums, True
    )
    far = [
        swapped(part, (targets[0][slot], targets[1][slot]))
        for slot, part in enumerate(sums)
    ]
    near, *taps = trial_sums(
        got, first(0, slots), sub_delay, sizes, both(0), [near], box_width=box_width
    )
    mine, *sends = cut_by_phase(near, far, blocks, trials, owners)
    got = [
        lax.ppermute(send, "tm", pairs(owners, flip + 1))
        for flip, send in enumerate(sends)
    ]
    return fold_and_box(mine, got, taps, periods, trials, owners)


def solution(mesh):
    placed = (P("chan", "tm"), P("chan"), P(), P())
    return jax.shard_map(
        per_device,
        mesh=mesh,
        in_specs=placed,
        out_specs=(P("chan", None, "tm"), P("chan", None, None, "tm")),
        check_vma=False,
    )
```

```python
import functools
import math

import jax
import jax.numpy as jnp
from jax import lax
from jax.experimental import pallas as pl
from jax.experimental.pallas import tpu as pltpu
from jax.sharding import PartitionSpec as P

NCHAN = 4096
NSUB = 64
NDM = 64
NBIN = 2048
LEVELS = 4
MAXW = 32
D1MAX = 128
D2MAX = 896

LANES = 128
F32 = jnp.float32
GROUP = 2**LEVELS
ROW_BLOCKS = NBIN // LANES
LEAD = (D1MAX + D2MAX) // LANES
VMEM_LIMIT = 48 << 20
SCALE = 2.0 ** (-LEVELS / 2) / math.sqrt(NCHAN)


def lane_iota(rows):
    return lax.broadcasted_iota(jnp.int32, (rows, LANES), 1)


def column_exponent(peak):
    return jnp.floor(jnp.log2(jnp.maximum(peak, 2.0**-110))) - 14.0


def scaled(values, exponent):
    return jnp.clip(jnp.round(values * jnp.exp2(-exponent)), -32767.0, 32767.0)


def to_i16(values):
    return values.astype(jnp.int32).astype(jnp.int16)


def pairs(size, flip):
    return [(i, i ^ flip) for i in range(size)]


def subband_kernel(chans, blocks, subs, delay_hbm, x_hbm, out_ref, *scratch):
    delay_ref, x_ref, turned, late, sums, x_sem, delay_sem = scratch
    delay_copy = pltpu.make_async_copy(delay_hbm, delay_ref, delay_sem)
    delay_copy.start()

    def x_copy(sub):
        return pltpu.make_async_copy(
            x_hbm.at[pl.ds(sub * chans, chans), :], x_ref.at[sub], x_sem.at[sub]
        )

    for sub in range(subs):
        x_copy(sub).start()
    delay_copy.wait()
    lane = lane_iota(8)
    tiles = blocks // 8
    pitch = blocks + 4

    @pl.loop(0, subs)
    def _(sub):
        x_copy(sub).wait()
        here = [jnp.zeros((8, LANES), F32)] * tiles
        before = [jnp.zeros((8, LANES), F32)] * tiles
        for octet in range(chans // 8):
            if octet % 2 == 0:
                for block in range(blocks):
                    both = x_ref[
                        sub,
                        8 * octet : 8 * octet + 16,
                        block * LANES : (block + 1) * LANES,
                    ].astype(F32)
                    for k in range(2):
                        base = (octet + k) * pitch * 8
                        if (octet + k) % 4 == 0:
                            at = pl.ds(base + block * 8, 8)
                        else:
                            at = pl.ds(base + block, 8, stride=pitch)
                        turned[at, :] = both[8 * k : 8 * k + 8]
            for i in range(8):
                delay = delay_ref[sub * chans + octet * 8 + i]
                shift = (2 * LANES - delay) & (LANES - 1)
                stays = lane < LANES - delay
                values = []
                for t in range(tiles):
                    base = octet * pitch * 8
                    if octet % 4 == 0:
                        at = pl.ds(base + t * 64 + i, 8, stride=8)
                    else:
                        at = pl.ds(base + i * pitch + t * 8, 8)
                    values.append(turned[at, :])
                for t in range(0, tiles, 2):
                    both = jnp.concatenate(values[t : t + 2], axis=0)
                    both = pltpu.roll(both.astype(x_ref.dtype), shift, 1).astype(F32)
                    for k in range(2):
                        value = both[8 * k : 8 * k + 8]
                        here[t + k] = here[t + k] + jnp.where(stays, value, 0.0)
                        before[t + k] = before[t + k] + jnp.where(stays, 0.0, value)
        for t in range(tiles):
            late[8 * t : 8 * t + 8, :] = before[t]
        late[blocks : blocks + 8, :] = jnp.zeros((8, LANES), F32)
        sums[pl.ds(sub, 1), :] = late[0:1, :]
        for t in range(tiles):
            sums[pl.ds((8 * t + 1) * subs + sub, 8, stride=subs), :] = (
                here[t] + late[8 * t + 1 : 8 * t + 9, :]
            )

    rows = (blocks + 1) * subs
    values = sums[...].reshape(blocks + 1, subs, LANES)
    exponent = column_exponent(jnp.max(jnp.abs(values), axis=0))
    out_ref[0:rows, :] = to_i16(scaled(values, exponent[None]).reshape(rows, LANES))
    out_ref[rows : rows + subs, :] = to_i16(exponent)


def subband_sums(filterbank, chan_delay, subs):
    chans_here, samples = filterbank.shape
    chans, blocks = chans_here // subs, samples // LANES
    rows = (blocks + 2) * subs
    return pl.pallas_call(
        functools.partial(subband_kernel, chans, blocks, subs),
        in_specs=[pl.BlockSpec(memory_space=pltpu.HBM)] * 2,
        out_specs=pl.BlockSpec(memory_space=pltpu.VMEM),
        out_shape=jax.ShapeDtypeStruct((rows, LANES), jnp.int16),
        scratch_shapes=[
            pltpu.SMEM((chans_here,), jnp.int32),
            pltpu.VMEM((subs, chans, samples), filterbank.dtype),
            pltpu.VMEM((chans * (blocks + 4), LANES), F32),
            pltpu.VMEM((blocks + 8, LANES), F32),
            pltpu.VMEM(((blocks + 1) * subs, LANES), F32),
            pltpu.SemaphoreType.DMA((subs,)),
            pltpu.SemaphoreType.DMA(()),
        ],
        compiler_params=pltpu.CompilerParams(vmem_limit_bytes=VMEM_LIMIT),
        name="subbands",
    )(pltpu.with_memory_space_constraint(chan_delay, pltpu.HBM), filterbank)


def box_taps(width_ref, band_ref, weight_ref):
    ahead = lax.broadcasted_iota(
        jnp.int32, (2 * LANES, LANES), 0
    ) - lax.broadcasted_iota(jnp.int32, (2 * LANES, LANES), 1)
    for w in range(width_ref.shape[0]):
        width = width_ref[w]
        inside = jnp.logical_and(ahead >= 0, ahead < width)
        inside = jnp.where(inside, 1.0, 0.0).astype(band_ref.dtype)
        band_ref[:, w * LANES : (w + 1) * LANES] = inside
        count = jnp.full((8, LANES), width, jnp.int32).astype(F32)
        weight_ref[8 * w : 8 * w + 8, :] = 1.0 / jnp.sqrt(count)


def trial_kernel(
    blocks, subs, trials, origins, flips, primed, coded, taps, delays, *refs
):
    refs = list(refs)
    take = lambda n: [refs.pop(0) for _ in range(n)]
    parts = take(len(origins))
    priors = take(len(flips)) if primed else []
    width_ref = take(1)[0] if taps else None
    outs = take(len(flips))
    if taps:
        box_taps(width_ref, *take(2))
    spread, late, acc, delay_ref, delay_sem = refs
    chan = lax.axis_index("chan")
    fetched = delay_ref.shape[1]
    copies, offset = [], []
    for i, flip in enumerate(flips):
        wanted = (chan ^ flip) * trials
        first = wanted // fetched * fetched
        offset.append(wanted - first)
        copies.append(
            pltpu.make_async_copy(
                delays.at[pl.ds(pl.multiple_of(first, 8), fetched), :],
                delay_ref.at[i],
                delay_sem.at[i],
            )
        )
        copies[i].start()
    out_blocks = LEAD + blocks
    depth = out_blocks + LEAD
    for at, part in enumerate(parts):
        base = at * depth * subs
        rows = (blocks + 1) * subs
        scale = jnp.exp2(part[rows : rows + subs, :].astype(F32))
        lead = (LEAD - 1) * subs
        spread[base : base + lead, :] = jnp.zeros((lead, LANES), F32)
        tail = base + lead + rows
        spread[tail : base + depth * subs, :] = jnp.zeros(
            (depth * subs - lead - rows, LANES), F32
        )
        values = part[0:rows, :].astype(F32).reshape(blocks + 1, subs, LANES)
        spread[base + lead : tail, :] = (values * scale[None]).reshape(rows, LANES)

    lane = lane_iota(8)
    tiles = out_blocks // 8

    for copy in copies:
        copy.wait()

    def one_trial(trial, i, prior, out):
        here = [jnp.zeros((8, LANES), F32)] * tiles
        before = [jnp.zeros((8, LANES), F32)] * tiles
        for at, origin in enumerate(origins):
            for sub in range(subs):
                delay = delay_ref[i, offset[i] + trial, (chan ^ origin) * subs + sub]
                shift = delay & (LANES - 1)
                stays = lane < LANES - shift
                back = (LANES - shift) & (LANES - 1)
                for t in range(tiles):
                    first = (at * depth + (delay >> 7) + 8 * t) * subs + sub
                    value = spread[pl.ds(first, 8, stride=subs), :]
                    value = pltpu.roll(value, back, 1)
                    here[t] = here[t] + jnp.where(stays, value, 0.0)
                    before[t] = before[t] + jnp.where(stays, 0.0, value)
        for t in range(tiles):
            late[8 * t : 8 * t + 8, :] = before[t]
        late[out_blocks : out_blocks + 8, :] = jnp.zeros((8, LANES), F32)
        for t in range(tiles):
            rows = pl.ds(8 * t * trials + trial, 8, stride=trials)
            value = here[t] + late[8 * t + 1 : 8 * t + 9, :]
            out[rows, :] = value if prior is None else value + prior[rows, :]

    rows = out_blocks * trials
    for i, (flip, out) in enumerate(zip(flips, outs)):
        target = acc if coded else out

        @pl.loop(0, trials, unroll=trials)
        def _(trial):
            one_trial(trial, i, priors[i] if primed else None, target)

        if coded:
            values = acc[...].reshape(out_blocks, trials, LANES)
            exponent = column_exponent(jnp.max(jnp.abs(values), axis=0))
            out[0:rows, :] = to_i16(
                scaled(values, exponent[None]).reshape(rows, LANES)
            )
            out[rows : rows + trials, :] = to_i16(exponent)


def trial_sums(
    parts, origins, sub_delay, sizes, flips, priors=None, coded=False, box_width=None
):
    if not flips:
        return []
    blocks, subs, trials = sizes
    out_blocks = LEAD + blocks
    depth = out_blocks + LEAD
    rows = out_blocks * trials
    out = jax.ShapeDtypeStruct(
        (rows + trials if coded else rows, LANES), jnp.int16 if coded else F32
    )
    vmem = pl.BlockSpec(memory_space=pltpu.VMEM)
    arrays = [*parts, *(priors or [])]
    in_specs = [pl.BlockSpec(memory_space=pl.ANY)] + [vmem] * len(arrays)
    outs = [out] * len(flips)
    taps = box_width is not None
    if taps:
        widths = box_width.shape[0]
        arrays.append(box_width)
        in_specs.append(pl.BlockSpec(memory_space=pltpu.SMEM))
        outs.append(jax.ShapeDtypeStruct((2 * LANES, widths * LANES), jnp.bfloat16))
        outs.append(jax.ShapeDtypeStruct((widths * 8, LANES), F32))
    return pl.pallas_call(
        functools.partial(
            trial_kernel, *sizes, tuple(origins), tuple(flips), bool(priors), coded, taps
        ),
        in_specs=in_specs,
        out_specs=[vmem] * len(outs),
        out_shape=outs,
        scratch_shapes=[
            pltpu.VMEM((len(parts) * depth * subs, LANES), F32),
            pltpu.VMEM((out_blocks + 8, LANES), F32),
            pltpu.VMEM((rows, LANES), F32),
            pltpu.SMEM((len(flips), max(trials, 8), sub_delay.shape[1]), jnp.int32),
            pltpu.SemaphoreType.DMA((len(flips),)),
        ],
        compiler_params=pltpu.CompilerParams(vmem_limit_bytes=VMEM_LIMIT),
        name="trials_coded" if coded else "trials",
    )(sub_delay, *arrays)


def cut_kernel(blocks, trials, owners, n_far, own_ref, *refs):
    far, mine, sends = refs[:n_far], refs[n_far], refs[n_far + 1 : n_far + owners]
    series, whole, piece = refs[n_far + owners :]
    here = lax.axis_index("tm")
    out_blocks = LEAD + blocks
    rows = out_blocks * trials
    total = own_ref[...].reshape(out_blocks, trials, LANES)
    for part in far:
        scale = jnp.exp2(part[rows : rows + trials, :].astype(F32))
        values = part[0:rows, :].astype(F32).reshape(out_blocks, trials, LANES)
        total = total + values * scale[None]
    total = total * SCALE
    ahead = (ROW_BLOCKS - LEAD) * trials
    exponent = column_exponent(jnp.max(jnp.abs(total), axis=0))
    for target, values in ((series, total), (whole, scaled(total, exponent[None]))):
        target[0:ahead, :] = jnp.zeros((ahead, LANES), F32)
        target[ahead : ahead + rows, :] = values.reshape(rows, LANES)
    periods = blocks // ROW_BLOCKS
    bin_blocks = ROW_BLOCKS // owners
    for flip in range(owners):
        source, target = (series, mine) if flip == 0 else (whole, piece)
        at = 0
        for period in range(periods + 1):
            for j in range(bin_blocks + 1):
                block = ((here ^ flip) * bin_blocks + j) & (ROW_BLOCKS - 1)
                first = (period * ROW_BLOCKS + block) * trials
                target[at : at + trials, :] = source[pl.ds(first, trials), :]
                at += trials
        if flip:
            sends[flip - 1][0:at, :] = to_i16(piece[...])
            sends[flip - 1][at : at + trials, :] = to_i16(exponent)


def cut_by_phase(own, far, blocks, trials, owners):
    out_blocks = LEAD + blocks
    periods = blocks // ROW_BLOCKS
    bin_blocks = ROW_BLOCKS // owners
    rows = (periods + 1) * (bin_blocks + 1) * trials
    vmem = pl.BlockSpec(memory_space=pltpu.VMEM)
    held = (out_blocks + ROW_BLOCKS - LEAD) * trials
    return pl.pallas_call(
        functools.partial(cut_kernel, blocks, trials, owners, len(far)),
        in_specs=[vmem] * (1 + len(far)),
        out_specs=[vmem] * owners,
        out_shape=[jax.ShapeDtypeStruct((rows, LANES), F32)]
        + [jax.ShapeDtypeStruct((rows + trials, LANES), jnp.int16)] * (owners - 1),
        scratch_shapes=[
            pltpu.VMEM((held, LANES), F32),
            pltpu.VMEM((held, LANES), F32),
            pltpu.VMEM((rows, LANES), F32),
        ],
        compiler_params=pltpu.CompilerParams(vmem_limit_bytes=VMEM_LIMIT),
        name="cut",
    )(own, *far)


def fold_kernel(periods, trials, owners, widths, band_ref, weight_ref, mine_ref, *refs):
    parts, (ffa_ref, box_ref) = refs[: owners - 1], refs[owners - 1 : owners + 1]
    rows_in, code, left = refs[owners + 1 :]
    here = lax.axis_index("tm")
    bin_blocks = ROW_BLOCKS // owners
    row_len = (bin_blocks + 1) * trials
    held = periods * row_len
    rows_in[0:row_len, :] = jnp.zeros((row_len, LANES), F32)
    for flip in range(owners):
        if flip == 0:
            rest = mine_ref[row_len : row_len + held, :]
        else:
            part = parts[flip - 1]
            total = row_len + held
            scale = jnp.exp2(part[total : total + trials, :].astype(F32))
            values = part[0:total, :].astype(F32)
            values = values.reshape(total // trials, trials, LANES) * scale[None]
            code[flip - 1] = values.reshape(total, LANES)
            rest = code[flip - 1, row_len : row_len + held, :]
        first = (here ^ flip) * held + row_len
        rows_in[pl.ds(first, held), :] = rest
    for flip in range(owners):
        early = mine_ref[0:row_len, :] if flip == 0 else code[flip - 1, 0:row_len, :]
        first = (here ^ flip) * held
        rows_in[pl.ds(first, row_len), :] += early

    band = band_ref[...]
    weights = [weight_ref[8 * w : 8 * w + trials, :] for w in range(widths)]
    lane = lane_iota(trials)
    row_count = owners * periods

    def moved(row, by):
        if by == 0:
            return row
        rolled = [pltpu.roll(block, LANES - by, 1) for block in row]
        out = []
        for b in range(bin_blocks + 1):
            after = rolled[min(b + 1, bin_blocks)]
            out.append(jnp.where(lane < LANES - by, rolled[b], after))
        return out

    for group in range(row_count // GROUP):
        rows = []
        for r in range(GROUP):
            at = (1 + group * GROUP + r) * row_len
            rows.append(
                [
                    rows_in[at + b * trials : at + (b + 1) * trials, :]
                    for b in range(bin_blocks + 1)
                ]
            )
        for level in range(LEVELS):
            half = 2**level
            new = []
            for start in range(0, GROUP, 2 * half):
                for j in range(2 * half):
                    upper = rows[start + j // 2]
                    lower = moved(rows[start + half + j // 2], (j + 1) // 2)
                    new.append([u + low for u, low in zip(upper, lower)])
            rows = new
        for r in range(GROUP):
            row = group * GROUP + r
            for b in range(bin_blocks):
                at = (r * bin_blocks + b) * trials
                left[at : at + trials, 0:LANES] = rows[r][b]
                left[at : at + trials, LANES : 2 * LANES] = rows[r][b + 1]
                first = (row // 8 * bin_blocks + b) * 8 + row % 8
                step = row_count * bin_blocks
                ffa_ref[pl.ds(first, trials, stride=step), :] = rows[r][b]
        rest = left[...]
        product = None
        for _ in range(2):
            high = rest.astype(jnp.bfloat16)
            rest = rest - high.astype(F32)
            term = jnp.dot(high, band, preferred_element_type=F32)
            product = term if product is None else product + term
        step = row_count * bin_blocks * widths
        for i in range(GROUP * bin_blocks):
            for w in range(widths):
                value = product[
                    i * trials : (i + 1) * trials, w * LANES : (w + 1) * LANES
                ]
                first = (group * GROUP * bin_blocks + i) * widths + w
                box_ref[pl.ds(first, trials, stride=step), :] = value * weights[w]


def fold_and_box(mine, parts, taps, periods, trials, owners):
    bin_blocks = ROW_BLOCKS // owners
    widths = taps[0].shape[1] // LANES
    row_count = owners * periods
    row_len = (bin_blocks + 1) * trials
    ffa_rows = trials * row_count * bin_blocks
    ffa_shape = jax.ShapeDtypeStruct((ffa_rows, LANES), F32)
    box_shape = jax.ShapeDtypeStruct((ffa_rows * widths, LANES), F32)
    vmem = pl.BlockSpec(memory_space=pltpu.VMEM)
    ffa, box = pl.pallas_call(
        functools.partial(fold_kernel, periods, trials, owners, widths),
        in_specs=[vmem] * (2 + owners),
        out_specs=[vmem, vmem],
        out_shape=[ffa_shape, box_shape],
        scratch_shapes=[
            pltpu.VMEM(((row_count + 1) * row_len, LANES), F32),
            pltpu.VMEM((max(owners - 1, 1), (periods + 1) * row_len, LANES), F32),
            pltpu.VMEM((GROUP * bin_blocks * trials, 2 * LANES), F32),
        ],
        compiler_params=pltpu.CompilerParams(vmem_limit_bytes=VMEM_LIMIT),
        name="fold",
    )(*taps, mine, *parts)
    bins = bin_blocks * LANES
    ffa = ffa.reshape(trials, row_count // 8, bin_blocks, 8, LANES)
    ffa = ffa.transpose(0, 1, 3, 2, 4).reshape(trials, row_count, bins)
    box = box.reshape(trials, row_count, bin_blocks, widths, LANES)
    box = box.transpose(0, 1, 3, 2, 4).reshape(trials, row_count, widths, bins)
    return ffa, box


def per_device(filterbank, chan_delay, sub_delay, box_width):
    chan_size, owners = lax.axis_size("chan"), lax.axis_size("tm")
    samples = filterbank.shape[1]
    subs, trials = NSUB // chan_size, NDM // chan_size
    blocks, periods = samples // LANES, samples // NBIN
    quad = math.gcd(chan_size, 4)
    own = subband_sums(filterbank, chan_delay, subs)
    part = {0: own}
    for flip in range(1, quad):
        part[flip] = lax.ppermute(own, "chan", pairs(chan_size, flip))
    sizes = (blocks, subs, trials)
    flips = tuple(range(quad, chan_size, quad))
    early, final = ((0, 2, 1), (3,)) if quad == 4 else ((0,), tuple(range(1, quad)))
    far, near = None, None
    for origin in early:
        both = origin == 0
        sums = trial_sums(
            [part[origin]], (origin,), sub_delay, sizes, (*flips, 0) if both else flips, far
        )
        far, near = (sums[:-1], sums[-1:]) if both else (sums, near)
    last = [part[origin] for origin in final]
    far = trial_sums(last, final, sub_delay, sizes, flips, far, True)
    far = [
        lax.ppermute(send, "chan", pairs(chan_size, flip))
        for send, flip in zip(far, flips)
    ]
    rest = (*early[1:], *final)
    near, *taps = trial_sums(
        [part[o] for o in rest], rest, sub_delay, sizes, (0,), near, box_width=box_width
    )
    mine, *sends = cut_by_phase(near, far, blocks, trials, owners)
    got = [
        lax.ppermute(send, "tm", pairs(owners, flip + 1))
        for flip, send in enumerate(sends)
    ]
    return fold_and_box(mine, got, taps, periods, trials, owners)


def solution(mesh):
    placed = (P("chan", "tm"), P("chan"), P(), P())
    return jax.shard_map(
        per_device,
        mesh=mesh,
        in_specs=placed,
        out_specs=(P("chan", None, "tm"), P("chan", None, None, "tm")),
        check_vma=False,
    )
```

```python
import functools
import math

import jax
import jax.numpy as jnp
from jax import lax
from jax.experimental import pallas as pl
from jax.experimental.pallas import tpu as pltpu
from jax.sharding import PartitionSpec as P

NCHAN = 4096
NSUB = 64
NDM = 64
NBIN = 2048
LEVELS = 4
MAXW = 32
D1MAX = 128
D2MAX = 896

LANES = 128
F32 = jnp.float32
GROUP = 2**LEVELS
ROW_BLOCKS = NBIN // LANES
LEAD = (D1MAX + D2MAX) // LANES
VMEM_LIMIT = 48 << 20
SCALE = 2.0 ** (-LEVELS / 2) / math.sqrt(NCHAN)


def lane_iota(rows):
    return lax.broadcasted_iota(jnp.int32, (rows, LANES), 1)


def column_exponent(peak):
    return jnp.floor(jnp.log2(jnp.maximum(peak, 2.0**-110))) - 14.0


def scaled(values, exponent):
    return jnp.clip(jnp.round(values * jnp.exp2(-exponent)), -32767.0, 32767.0)


def to_i16(values):
    return values.astype(jnp.int32).astype(jnp.int16)


def pairs(size, flip):
    return [(i, i ^ flip) for i in range(size)]


def subband_kernel(chans, blocks, subs, delay_hbm, x_hbm, out_ref, *scratch):
    delay_ref, x_ref, turned, late, sums, x_sem, delay_sem = scratch
    delay_copy = pltpu.make_async_copy(delay_hbm, delay_ref, delay_sem)
    delay_copy.start()

    def x_copy(sub):
        return pltpu.make_async_copy(
            x_hbm.at[pl.ds(sub * chans, chans), :], x_ref.at[sub], x_sem.at[sub]
        )

    for sub in range(subs):
        x_copy(sub).start()
    delay_copy.wait()
    lane = lane_iota(8)
    tiles = blocks // 8
    pitch = blocks + 4

    @pl.loop(0, subs)
    def _(sub):
        x_copy(sub).wait()
        here = [jnp.zeros((8, LANES), F32)] * tiles
        before = [jnp.zeros((8, LANES), F32)] * tiles
        for octet in range(chans // 8):
            if octet % 2 == 0:
                for block in range(blocks):
                    both = x_ref[
                        sub,
                        8 * octet : 8 * octet + 16,
                        block * LANES : (block + 1) * LANES,
                    ].astype(F32)
                    for k in range(2):
                        base = (octet + k) * pitch * 8
                        if (octet + k) % 4 == 0:
                            at = pl.ds(base + block * 8, 8)
                        else:
                            at = pl.ds(base + block, 8, stride=pitch)
                        turned[at, :] = both[8 * k : 8 * k + 8]
            for i in range(8):
                delay = delay_ref[sub * chans + octet * 8 + i]
                shift = (2 * LANES - delay) & (LANES - 1)
                stays = lane < LANES - delay
                values = []
                for t in range(tiles):
                    base = octet * pitch * 8
                    if octet % 4 == 0:
                        at = pl.ds(base + t * 64 + i, 8, stride=8)
                    else:
                        at = pl.ds(base + i * pitch + t * 8, 8)
                    values.append(turned[at, :])
                for t in range(0, tiles, 2):
                    both = jnp.concatenate(values[t : t + 2], axis=0)
                    both = pltpu.roll(both.astype(x_ref.dtype), shift, 1).astype(F32)
                    for k in range(2):
                        value = both[8 * k : 8 * k + 8]
                        here[t + k] = here[t + k] + jnp.where(stays, value, 0.0)
                        before[t + k] = before[t + k] + jnp.where(stays, 0.0, value)
        for t in range(tiles):
            late[8 * t : 8 * t + 8, :] = before[t]
        late[blocks : blocks + 8, :] = jnp.zeros((8, LANES), F32)
        sums[pl.ds(sub, 1), :] = late[0:1, :]
        for t in range(tiles):
            sums[pl.ds((8 * t + 1) * subs + sub, 8, stride=subs), :] = (
                here[t] + late[8 * t + 1 : 8 * t + 9, :]
            )

    rows = (blocks + 1) * subs
    values = sums[...].reshape(blocks + 1, subs, LANES)
    exponent = column_exponent(jnp.max(jnp.abs(values), axis=0))
    out_ref[0:rows, :] = to_i16(scaled(values, exponent[None]).reshape(rows, LANES))
    out_ref[rows : rows + subs, :] = to_i16(exponent)


def subband_sums(filterbank, chan_delay, subs):
    chans_here, samples = filterbank.shape
    chans, blocks = chans_here // subs, samples // LANES
    rows = (blocks + 2) * subs
    return pl.pallas_call(
        functools.partial(subband_kernel, chans, blocks, subs),
        in_specs=[pl.BlockSpec(memory_space=pltpu.HBM)] * 2,
        out_specs=pl.BlockSpec(memory_space=pltpu.VMEM),
        out_shape=jax.ShapeDtypeStruct((rows, LANES), jnp.int16),
        scratch_shapes=[
            pltpu.SMEM((chans_here,), jnp.int32),
            pltpu.VMEM((subs, chans, samples), filterbank.dtype),
            pltpu.VMEM((chans * (blocks + 4), LANES), F32),
            pltpu.VMEM((blocks + 8, LANES), F32),
            pltpu.VMEM(((blocks + 1) * subs, LANES), F32),
            pltpu.SemaphoreType.DMA((subs,)),
            pltpu.SemaphoreType.DMA(()),
        ],
        compiler_params=pltpu.CompilerParams(vmem_limit_bytes=VMEM_LIMIT),
        name="subbands",
    )(pltpu.with_memory_space_constraint(chan_delay, pltpu.HBM), filterbank)


def box_taps(width_ref, band_ref, weight_ref):
    ahead = lax.broadcasted_iota(
        jnp.int32, (2 * LANES, LANES), 0
    ) - lax.broadcasted_iota(jnp.int32, (2 * LANES, LANES), 1)
    for w in range(width_ref.shape[0]):
        width = width_ref[w]
        inside = jnp.logical_and(ahead >= 0, ahead < width)
        inside = jnp.where(inside, 1.0, 0.0).astype(band_ref.dtype)
        band_ref[:, w * LANES : (w + 1) * LANES] = inside
        count = jnp.full((8, LANES), width, jnp.int32).astype(F32)
        weight_ref[8 * w : 8 * w + 8, :] = 1.0 / jnp.sqrt(count)


def trial_kernel(
    blocks, subs, trials, origins, flips, primed, coded, taps, delays, *refs
):
    refs = list(refs)
    take = lambda n: [refs.pop(0) for _ in range(n)]
    parts = take(len(origins))
    priors = take(len(flips)) if primed else []
    width_ref = take(1)[0] if taps else None
    outs = take(len(flips))
    if taps:
        box_taps(width_ref, *take(2))
    spread, late, acc, delay_ref, delay_sem = refs
    chan = lax.axis_index("chan")
    fetched = delay_ref.shape[1]
    copies, offset = [], []
    for i, flip in enumerate(flips):
        wanted = (chan ^ flip) * trials
        first = wanted // fetched * fetched
        offset.append(wanted - first)
        copies.append(
            pltpu.make_async_copy(
                delays.at[pl.ds(pl.multiple_of(first, 8), fetched), :],
                delay_ref.at[i],
                delay_sem.at[i],
            )
        )
        copies[i].start()
    out_blocks = LEAD + blocks
    depth = out_blocks + LEAD
    for at, part in enumerate(parts):
        base = at * depth * subs
        rows = (blocks + 1) * subs
        scale = jnp.exp2(part[rows : rows + subs, :].astype(F32))
        lead = (LEAD - 1) * subs
        spread[base : base + lead, :] = jnp.zeros((lead, LANES), F32)
        tail = base + lead + rows
        spread[tail : base + depth * subs, :] = jnp.zeros(
            (depth * subs - lead - rows, LANES), F32
        )
        values = part[0:rows, :].astype(F32).reshape(blocks + 1, subs, LANES)
        spread[base + lead : tail, :] = (values * scale[None]).reshape(rows, LANES)

    lane = lane_iota(8)
    tiles = out_blocks // 8

    for copy in copies:
        copy.wait()

    def one_trial(trial, i, prior, out):
        here = [jnp.zeros((8, LANES), F32)] * tiles
        before = [jnp.zeros((8, LANES), F32)] * tiles
        for at, origin in enumerate(origins):
            for sub in range(subs):
                delay = delay_ref[i, offset[i] + trial, (chan ^ origin) * subs + sub]
                shift = delay & (LANES - 1)
                stays = lane < LANES - shift
                back = (LANES - shift) & (LANES - 1)
                for t in range(tiles):
                    first = (at * depth + (delay >> 7) + 8 * t) * subs + sub
                    value = spread[pl.ds(first, 8, stride=subs), :]
                    value = pltpu.roll(value, back, 1)
                    here[t] = here[t] + jnp.where(stays, value, 0.0)
                    before[t] = before[t] + jnp.where(stays, 0.0, value)
        for t in range(tiles):
            late[8 * t : 8 * t + 8, :] = before[t]
        late[out_blocks : out_blocks + 8, :] = jnp.zeros((8, LANES), F32)
        for t in range(tiles):
            rows = pl.ds(8 * t * trials + trial, 8, stride=trials)
            value = here[t] + late[8 * t + 1 : 8 * t + 9, :]
            out[rows, :] = value if prior is None else value + prior[rows, :]

    rows = out_blocks * trials
    for i, (flip, out) in enumerate(zip(flips, outs)):
        target = acc if coded else out

        @pl.loop(0, trials, unroll=trials)
        def _(trial):
            one_trial(trial, i, priors[i] if primed else None, target)

        if coded:
            values = acc[...].reshape(out_blocks, trials, LANES)
            exponent = column_exponent(jnp.max(jnp.abs(values), axis=0))
            out[0:rows, :] = to_i16(
                scaled(values, exponent[None]).reshape(rows, LANES)
            )
            out[rows : rows + trials, :] = to_i16(exponent)


def trial_sums(
    parts, origins, sub_delay, sizes, flips, priors=None, coded=False, box_width=None
):
    if not flips:
        return []
    blocks, subs, trials = sizes
    out_blocks = LEAD + blocks
    depth = out_blocks + LEAD
    rows = out_blocks * trials
    out = jax.ShapeDtypeStruct(
        (rows + trials if coded else rows, LANES), jnp.int16 if coded else F32
    )
    vmem = pl.BlockSpec(memory_space=pltpu.VMEM)
    arrays = [*parts, *(priors or [])]
    in_specs = [pl.BlockSpec(memory_space=pl.ANY)] + [vmem] * len(arrays)
    outs = [out] * len(flips)
    taps = box_width is not None
    if taps:
        widths = box_width.shape[0]
        arrays.append(box_width)
        in_specs.append(pl.BlockSpec(memory_space=pltpu.SMEM))
        outs.append(jax.ShapeDtypeStruct((2 * LANES, widths * LANES), jnp.bfloat16))
        outs.append(jax.ShapeDtypeStruct((widths * 8, LANES), F32))
    return pl.pallas_call(
        functools.partial(
            trial_kernel, *sizes, tuple(origins), tuple(flips), bool(priors), coded, taps
        ),
        in_specs=in_specs,
        out_specs=[vmem] * len(outs),
        out_shape=outs,
        scratch_shapes=[
            pltpu.VMEM((len(parts) * depth * subs, LANES), F32),
            pltpu.VMEM((out_blocks + 8, LANES), F32),
            pltpu.VMEM((rows, LANES), F32),
            pltpu.SMEM((len(flips), max(trials, 8), sub_delay.shape[1]), jnp.int32),
            pltpu.SemaphoreType.DMA((len(flips),)),
        ],
        compiler_params=pltpu.CompilerParams(vmem_limit_bytes=VMEM_LIMIT),
        name="trials_coded" if coded else "trials",
    )(sub_delay, *arrays)


def cut_kernel(blocks, trials, owners, n_far, own_ref, *refs):
    far, mine, sends = refs[:n_far], refs[n_far], refs[n_far + 1 : n_far + owners]
    series, whole, piece = refs[n_far + owners :]
    here = lax.axis_index("tm")
    out_blocks = LEAD + blocks
    rows = out_blocks * trials
    total = own_ref[...].reshape(out_blocks, trials, LANES)
    for part in far:
        scale = jnp.exp2(part[rows : rows + trials, :].astype(F32))
        values = part[0:rows, :].astype(F32).reshape(out_blocks, trials, LANES)
        total = total + values * scale[None]
    total = total * SCALE
    ahead = (ROW_BLOCKS - LEAD) * trials
    exponent = column_exponent(jnp.max(jnp.abs(total), axis=0))
    for target, values in ((series, total), (whole, scaled(total, exponent[None]))):
        target[0:ahead, :] = jnp.zeros((ahead, LANES), F32)
        target[ahead : ahead + rows, :] = values.reshape(rows, LANES)
    periods = blocks // ROW_BLOCKS
    bin_blocks = ROW_BLOCKS // owners
    for flip in range(owners):
        source, target = (series, mine) if flip == 0 else (whole, piece)
        at = 0
        for period in range(periods + 1):
            for j in range(bin_blocks + 1):
                block = ((here ^ flip) * bin_blocks + j) & (ROW_BLOCKS - 1)
                first = (period * ROW_BLOCKS + block) * trials
                target[at : at + trials, :] = source[pl.ds(first, trials), :]
                at += trials
        if flip:
            sends[flip - 1][0:at, :] = to_i16(piece[...])
            sends[flip - 1][at : at + trials, :] = to_i16(exponent)


def cut_by_phase(own, far, blocks, trials, owners):
    out_blocks = LEAD + blocks
    periods = blocks // ROW_BLOCKS
    bin_blocks = ROW_BLOCKS // owners
    rows = (periods + 1) * (bin_blocks + 1) * trials
    vmem = pl.BlockSpec(memory_space=pltpu.VMEM)
    held = (out_blocks + ROW_BLOCKS - LEAD) * trials
    return pl.pallas_call(
        functools.partial(cut_kernel, blocks, trials, owners, len(far)),
        in_specs=[vmem] * (1 + len(far)),
        out_specs=[vmem] * owners,
        out_shape=[jax.ShapeDtypeStruct((rows, LANES), F32)]
        + [jax.ShapeDtypeStruct((rows + trials, LANES), jnp.int16)] * (owners - 1),
        scratch_shapes=[
            pltpu.VMEM((held, LANES), F32),
            pltpu.VMEM((held, LANES), F32),
            pltpu.VMEM((rows, LANES), F32),
        ],
        compiler_params=pltpu.CompilerParams(vmem_limit_bytes=VMEM_LIMIT),
        name="cut",
    )(own, *far)


def fold_kernel(periods, trials, owners, widths, band_ref, weight_ref, mine_ref, *refs):
    parts, (ffa_ref, box_ref) = refs[: owners - 1], refs[owners - 1 : owners + 1]
    rows_in, code, left = refs[owners + 1 :]
    here = lax.axis_index("tm")
    bin_blocks = ROW_BLOCKS // owners
    row_len = (bin_blocks + 1) * trials
    held = periods * row_len
    rows_in[0:row_len, :] = jnp.zeros((row_len, LANES), F32)
    for flip in range(owners):
        if flip == 0:
            rest = mine_ref[row_len : row_len + held, :]
        else:
            part = parts[flip - 1]
            total = row_len + held
            scale = jnp.exp2(part[total : total + trials, :].astype(F32))
            values = part[0:total, :].astype(F32)
            values = values.reshape(total // trials, trials, LANES) * scale[None]
            code[flip - 1] = values.reshape(total, LANES)
            rest = code[flip - 1, row_len : row_len + held, :]
        first = (here ^ flip) * held + row_len
        rows_in[pl.ds(first, held), :] = rest
    for flip in range(owners):
        early = mine_ref[0:row_len, :] if flip == 0 else code[flip - 1, 0:row_len, :]
        first = (here ^ flip) * held
        rows_in[pl.ds(first, row_len), :] += early

    band = band_ref[...]
    weights = [weight_ref[8 * w : 8 * w + trials, :] for w in range(widths)]
    lane = lane_iota(trials)
    row_count = owners * periods

    def moved(row, by):
        if by == 0:
            return row
        rolled = [pltpu.roll(block, LANES - by, 1) for block in row]
        out = []
        for b in range(bin_blocks + 1):
            after = rolled[min(b + 1, bin_blocks)]
            out.append(jnp.where(lane < LANES - by, rolled[b], after))
        return out

    for group in range(row_count // GROUP):
        rows = []
        for r in range(GROUP):
            at = (1 + group * GROUP + r) * row_len
            rows.append(
                [
                    rows_in[at + b * trials : at + (b + 1) * trials, :]
                    for b in range(bin_blocks + 1)
                ]
            )
        for level in range(LEVELS):
            half = 2**level
            new = []
            for start in range(0, GROUP, 2 * half):
                for j in range(2 * half):
                    upper = rows[start + j // 2]
                    lower = moved(rows[start + half + j // 2], (j + 1) // 2)
                    new.append([u + low for u, low in zip(upper, lower)])
            rows = new
        for r in range(GROUP):
            row = group * GROUP + r
            for b in range(bin_blocks):
                at = (r * bin_blocks + b) * trials
                left[at : at + trials, 0:LANES] = rows[r][b]
                left[at : at + trials, LANES : 2 * LANES] = rows[r][b + 1]
                first = (row // 8 * bin_blocks + b) * 8 + row % 8
                step = row_count * bin_blocks
                ffa_ref[pl.ds(first, trials, stride=step), :] = rows[r][b]
        rest = left[...]
        product = None
        for _ in range(2):
            high = rest.astype(jnp.bfloat16)
            rest = rest - high.astype(F32)
            term = jnp.dot(high, band, preferred_element_type=F32)
            product = term if product is None else product + term
        step = row_count * bin_blocks * widths
        for i in range(GROUP * bin_blocks):
            for w in range(widths):
                value = product[
                    i * trials : (i + 1) * trials, w * LANES : (w + 1) * LANES
                ]
                first = (group * GROUP * bin_blocks + i) * widths + w
                box_ref[pl.ds(first, trials, stride=step), :] = value * weights[w]


def fold_and_box(mine, parts, taps, periods, trials, owners):
    bin_blocks = ROW_BLOCKS // owners
    widths = taps[0].shape[1] // LANES
    row_count = owners * periods
    row_len = (bin_blocks + 1) * trials
    ffa_rows = trials * row_count * bin_blocks
    ffa_shape = jax.ShapeDtypeStruct((ffa_rows, LANES), F32)
    box_shape = jax.ShapeDtypeStruct((ffa_rows * widths, LANES), F32)
    vmem = pl.BlockSpec(memory_space=pltpu.VMEM)
    ffa, box = pl.pallas_call(
        functools.partial(fold_kernel, periods, trials, owners, widths),
        in_specs=[vmem] * (2 + owners),
        out_specs=[vmem, vmem],
        out_shape=[ffa_shape, box_shape],
        scratch_shapes=[
            pltpu.VMEM(((row_count + 1) * row_len, LANES), F32),
            pltpu.VMEM((max(owners - 1, 1), (periods + 1) * row_len, LANES), F32),
            pltpu.VMEM((GROUP * bin_blocks * trials, 2 * LANES), F32),
        ],
        compiler_params=pltpu.CompilerParams(vmem_limit_bytes=VMEM_LIMIT),
        name="fold",
    )(*taps, mine, *parts)
    bins = bin_blocks * LANES
    ffa = ffa.reshape(trials, row_count // 8, bin_blocks, 8, LANES)
    ffa = ffa.transpose(0, 1, 3, 2, 4).reshape(trials, row_count, bins)
    box = box.reshape(trials, row_count, bin_blocks, widths, LANES)
    box = box.transpose(0, 1, 3, 2, 4).reshape(trials, row_count, widths, bins)
    return ffa, box


def per_device(filterbank, chan_delay, sub_delay, box_width):
    chan_size, owners = lax.axis_size("chan"), lax.axis_size("tm")
    samples = filterbank.shape[1]
    subs, trials = NSUB // chan_size, NDM // chan_size
    blocks, periods = samples // LANES, samples // NBIN
    quad = math.gcd(chan_size, 4)
    own = subband_sums(filterbank, chan_delay, subs)
    part = {0: own}
    for flip in range(1, quad):
        part[flip] = lax.ppermute(own, "chan", pairs(chan_size, flip))
    sizes = (blocks, subs, trials)
    flips = tuple(range(quad, chan_size, quad))
    early, final = ((0, 2, 1), (3,)) if quad == 4 else ((0,), tuple(range(1, quad)))
    far = None
    for origin in early:
        far = trial_sums([part[origin]], (origin,), sub_delay, sizes, flips, far)
    last = [part[origin] for origin in final]
    far = trial_sums(last, final, sub_delay, sizes, flips, far, True)
    far = [
        lax.ppermute(send, "chan", pairs(chan_size, flip))
        for send, flip in zip(far, flips)
    ]
    rest = (*early, *final)
    near, *taps = trial_sums(
        [part[o] for o in rest], rest, sub_delay, sizes, (0,), box_width=box_width
    )
    mine, *sends = cut_by_phase(near, far, blocks, trials, owners)
    got = [
        lax.ppermute(send, "tm", pairs(owners, flip + 1))
        for flip, send in enumerate(sends)
    ]
    return fold_and_box(mine, got, taps, periods, trials, owners)


def solution(mesh):
    placed = (P("chan", "tm"), P("chan"), P(), P())
    return jax.shard_map(
        per_device,
        mesh=mesh,
        in_specs=placed,
        out_specs=(P("chan", None, "tm"), P("chan", None, None, "tm")),
        check_vma=False,
    )
```
